32 devices in a mesh: dp: 8 (over y, x, core), mp: 4 (over z).
Axes of the slice: x: 2, y: 2, z: 4, core: 2. Of those that a mesh axis runs over, the one named last changes fastest.
Arguments:
- tokens: bfloat16 [8192, 4096], P(('dp', 'mp')), may hold values from -600 to 600
- norm_gain: float32 [4096], replicated, may hold values from 0.5 to 2
- query_weight: bfloat16 [4096, 4096], P(None, 'mp'), may hold values from -0.09375 to 0.09375
- output_weight: bfloat16 [4096, 4096], P('mp'), may hold values from -0.75 to 0.75
- key_cache: bfloat16 [64, 128, 4096], P('dp', None, 'mp'), may hold values from -72 to 72
- value_cache: bfloat16 [64, 128, 4096], P('dp', None, 'mp'), may hold values from -6 to 6
- owners: int32 [128, 2], P('dp'), may hold values from 0 to 7, as said below
- slot_ids: int32 [128, 2], P('dp'), may hold values from 0 to 7
- valid_counts: int32 [128], P('dp'), may hold values from 0 to 2
Outputs:
- cross_out: bfloat16 [8192, 4096], P(('dp', 'mp'))
The draws below stay inside these ranges and needn't reach their ends.
Inputs may be any that keep to these rules, and one draw needn't show every extreme that they name: `owners`: each index of dp lists 2 x 16 neighbours; at most 4 of them lie with one owner, and one owner holds exactly 4 of the listed neighbours of every index of dp.
All inputs are finite; a program needn't handle non-finite values.
Results may differ from the reference program's by a relative error of at most 0.023.
Values may be sent and summed in bfloat16 or wider, within the bound.
No kernel may reach another device: no remote copies, remote signals or barrier semaphores. Data moves between devices by JAX's collectives and lax.ppermute only.
A program may use at most 128 MiB of HBM per device.

```python
import math
import jax
import jax.numpy as jnp
from jax import lax

D = 4096
H = 32
HD = 128
M = 64
NL = 128
SEQ = 1024
SLOTS = 8
CH = 16
SPANS = 128
DBS = 64
N_DP = 8
N_MP = 4


def draw_tokens(key, part):
    row_count = N_DP * SEQ
    row_scale = jnp.exp(jax.random.uniform(jax.random.fold_in(key, 1), (row_count, 1), jnp.float32, 0.0, math.log(10.0)))
    column_scale = jnp.exp(jax.random.uniform(jax.random.fold_in(key, 2), (1, D), jnp.float32, 0.0, math.log(10.0)))
    core = jnp.clip(jax.random.normal(jax.random.fold_in(key, 3), (row_count, D), jnp.float32), -6.0, 6.0)
    return (row_scale * column_scale * core).astype(jnp.bfloat16)


def draw_key_cache(key, part):
    block_count = N_DP * SLOTS
    return jnp.clip(jax.random.normal(jax.random.fold_in(key, 1), (block_count, NL, D), jnp.float32), -6.0, 6.0).astype(jnp.bfloat16)


def draw_owners(key, part):
    base_key = jax.random.fold_in(key, 11)
    neighbours = 2 * CH
    capacity = max(2, (neighbours + N_DP - 1) // N_DP)
    hot_owner = jax.random.randint(jax.random.fold_in(base_key, 1), (), 0, N_DP)
    others = (hot_owner + 1 + jnp.arange(N_DP - 1, dtype=jnp.int32)) % N_DP
    repeated = jnp.repeat(others, capacity)

    def one_list(group_index):
        list_key = jax.random.fold_in(base_key, group_index + 2)
        mixing = jax.random.permutation(jax.random.fold_in(list_key, 0), (N_DP - 1) * capacity)
        picked = repeated[mixing[:neighbours - capacity]]
        listing = jnp.concatenate([jnp.full((capacity,), hot_owner, jnp.int32), picked.astype(jnp.int32)])
        shuffle = jax.random.permutation(jax.random.fold_in(list_key, 1), neighbours)
        return listing[shuffle]
    lists = jax.vmap(one_list)(jnp.arange(N_DP, dtype=jnp.int32))
    return lists.reshape(N_DP * CH, 2).astype(jnp.int32)


def set_ends(drawn, stream_key, smallest, high):
    index_at = [jax.random.randint(jax.random.fold_in(stream_key, axis), (), 0, length) for axis, length in enumerate(drawn.shape)]
    widest = drawn.shape.index(max(drawn.shape))
    neighbour = index_at[:widest] + [(index_at[widest] + 1) % drawn.shape[widest]] + index_at[widest + 1:]
    return drawn.at[tuple(index_at)].set(smallest).at[tuple(neighbour)].set(high)


def level_of(stream_key, extent, split, low, largest):
    factor_of, own = 1.0, jax.random.fold_in(stream_key, 6)
    for dim, shards_of in split:
        steps = jnp.exp(jax.random.uniform(jax.random.fold_in(own, dim), (shards_of,), jnp.float32, low / len(split), largest / len(split)))
        factor_of = factor_of * jnp.repeat(steps, extent[dim] // shards_of).reshape([-1 if axis == dim else 1 for axis in range(len(extent))])
    return factor_of


def gaussian(own_key, extent, spread, bound, pieces=(), kind=jnp.bfloat16):
    values = jax.random.normal(own_key, extent, jnp.float32) * spread
    if len(pieces) > 0:
        values = level_of(own_key, extent, pieces, -0.22, 0.18) * values
    return jnp.clip(values, min=-bound, max=bound).astype(kind)


def setup_inputs(seed: int = 0) -> dict:
    splits = jax.random.split(jax.random.key(seed), 10)
    return {
        "tokens": draw_tokens(jax.random.fold_in(splits[9], 71), 0),
        "norm_gain": jnp.clip(jnp.exp(jax.random.uniform(splits[1], (D,), jnp.float32, math.log(0.5), math.log(2.0))), 0.5, 2.0),
        "query_weight": gaussian(splits[2], (D, D), D ** -0.5, 0.09375, ((1, 4),)),
        "output_weight": gaussian(splits[3], (D, D), (D // 64) ** -0.5, 0.75, ((0, 4),)),
        "key_cache": draw_key_cache(jax.random.fold_in(splits[9], 71), 0),
        "value_cache": gaussian(splits[5], (DBS, NL, D), 1.0, 6.0, ((0, 8), (2, 4))),
        "owners": draw_owners(jax.random.fold_in(splits[9], 71), 0),
        "slot_ids": set_ends(jax.random.randint(splits[7], (SPANS, 2), 0, SLOTS), jax.random.fold_in(splits[7], 1), 0, SLOTS - 1).astype(jnp.int32),
        "valid_counts": set_ends(jax.random.randint(splits[8], (SPANS,), 0, 3), jax.random.fold_in(splits[8], 1), 0, 2).astype(jnp.int32),
    }


def layer_norm(token_rows, norm_gain):
    values = token_rows.astype(jnp.float32)
    row_mean = lax.optimization_barrier(jnp.mean(values, axis=-1, keepdims=True))
    centered = values - row_mean
    variance = lax.optimization_barrier(jnp.mean(centered * centered, axis=-1, keepdims=True))
    return (centered * lax.rsqrt(variance + 1e-05) * norm_gain).astype(jnp.bfloat16)

def attend(queries, key_blocks, value_blocks, valid_counts, head_count):
    spans, length, local_width = queries.shape
    head_size = local_width // head_count
    query_heads = queries.reshape(spans, length, head_count, head_size).astype(jnp.float32)
    key_heads = key_blocks.reshape(spans, -1, head_count, head_size).astype(jnp.float32)
    value_heads = value_blocks.reshape(spans, -1, head_count, head_size).astype(jnp.float32)
    scores = jnp.einsum('cmhd,ckhd->chmk', query_heads, key_heads)
    usable = (jnp.arange(key_heads.shape[1], dtype=jnp.int32) // NL)[None, :] < valid_counts[:, None]
    usable = usable[:, None, None, :]
    masked = jnp.where(usable, scores, -1e+30)
    highest = lax.optimization_barrier(jnp.max(masked, axis=-1, keepdims=True))
    weights = jnp.where(usable, jnp.exp(masked - highest), 0.0)
    totals = lax.optimization_barrier(jnp.sum(weights, axis=-1)) + (valid_counts == 0).astype(jnp.float32)[:, None, None]
    rounded = lax.optimization_barrier(weights.astype(jnp.bfloat16)).astype(jnp.float32)
    mixture = jnp.einsum('chmk,ckhd->cmhd', rounded, value_heads)
    mixture = mixture / jnp.transpose(totals, (0, 2, 1))[..., None]
    return mixture.reshape(spans, length, local_width).astype(jnp.bfloat16)

def reference(tokens, norm_gain, query_weight, output_weight, key_cache, value_cache, owners, slot_ids, valid_counts):
    local_width = D // N_MP
    score_scale = 1.0 / math.sqrt(HD)

    def one_group(group_index):
        token_rows = lax.dynamic_slice_in_dim(tokens, group_index * SEQ, SEQ, 0)
        normed = layer_norm(token_rows, norm_gain)
        queries = (jnp.dot(normed, query_weight, preferred_element_type=jnp.float32) * score_scale).astype(jnp.bfloat16)
        shifted = jnp.concatenate([queries[M - 1:], jnp.zeros((M - 1, D), jnp.bfloat16)], axis=0).reshape(CH, M, D)
        group_owner = lax.dynamic_slice_in_dim(owners, group_index * CH, CH, 0)
        group_slot = lax.dynamic_slice_in_dim(slot_ids, group_index * CH, CH, 0)
        group_count = lax.dynamic_slice_in_dim(valid_counts, group_index * CH, CH, 0)
        block_index = (group_owner * SLOTS + group_slot).reshape(-1).astype(jnp.int32)
        key_blocks = jnp.take(key_cache, block_index, axis=0).reshape(CH, 2 * NL, D)
        value_blocks = jnp.take(value_cache, block_index, axis=0).reshape(CH, 2 * NL, D)
        attended = attend(shifted, key_blocks, value_blocks, group_count, H).reshape(SEQ, D)
        attended = jnp.concatenate([jnp.zeros((M - 1, D), jnp.bfloat16), attended[:SEQ - M + 1]], axis=0)
        summed = jnp.zeros((SEQ, D), jnp.float32)
        for member in range(N_MP):
            part_sum = jnp.dot(attended[:, member * local_width:(member + 1) * local_width], output_weight[member * local_width:(member + 1) * local_width], preferred_element_type=jnp.float32)
            summed = summed + lax.optimization_barrier(part_sum.astype(jnp.bfloat16)).astype(jnp.float32)
        return summed.astype(jnp.bfloat16)
    stacked = lax.map(one_group, jnp.arange(N_DP, dtype=jnp.int32))
    return stacked.reshape(N_DP * SEQ, D)
```

```python
import functools
import math

import jax
import jax.numpy as jnp
from jax import lax
from jax.experimental import pallas as pl
from jax.experimental.pallas import tpu as pltpu
from jax.sharding import PartitionSpec as P

HD = 128
M = 64
NL = 128


def layer_norm(token_rows, norm_gain):
    values = token_rows.astype(jnp.float32)
    row_mean = jnp.mean(values, axis=-1, keepdims=True)
    centered = values - row_mean
    variance = jnp.mean(centered * centered, axis=-1, keepdims=True)
    return (centered * lax.rsqrt(variance + 1e-05) * norm_gain).astype(jnp.bfloat16)


def span_attention(queries, key_blocks, value_blocks, valid_counts, head_count):
    spans, length, local_width = queries.shape
    query_heads = queries.reshape(spans, length, head_count, HD)
    key_heads = key_blocks.reshape(spans, -1, head_count, HD)
    value_heads = value_blocks.reshape(spans, -1, head_count, HD)
    scores = jnp.einsum(
        "cmhd,ckhd->chmk", query_heads, key_heads, preferred_element_type=jnp.float32
    )
    usable = (jnp.arange(key_heads.shape[1], dtype=jnp.int32) // NL)[None, :] < valid_counts[
        :, None
    ]
    usable = usable[:, None, None, :]
    masked = jnp.where(usable, scores, -1e30)
    highest = jnp.max(masked, axis=-1, keepdims=True)
    weights = jnp.where(usable, jnp.exp(masked - highest), 0.0)
    totals = jnp.sum(weights, axis=-1) + (valid_counts == 0).astype(jnp.float32)[:, None, None]
    mixture = jnp.einsum(
        "chmk,ckhd->cmhd",
        weights.astype(jnp.bfloat16),
        value_heads,
        preferred_element_type=jnp.float32,
    )
    mixture = mixture / jnp.transpose(totals, (0, 2, 1))[..., None]
    return mixture.reshape(spans, length, local_width).astype(jnp.bfloat16)


def general_on_device(
    tokens,
    norm_gain,
    query_weight,
    output_weight,
    key_cache,
    value_cache,
    owners,
    slot_ids,
    valid_counts,
):
    dp_count = lax.axis_size("dp")
    local_width = query_weight.shape[1]
    head_count = local_width // HD
    spans = valid_counts.shape[0]
    neighbours = 2 * spans
    capacity = max(2, (neighbours + dp_count - 1) // dp_count)
    score_scale = 1.0 / math.sqrt(HD)
    normed = layer_norm(tokens, norm_gain)
    queries = (
        jnp.dot(
            lax.all_gather(normed, "mp", axis=0, tiled=True),
            query_weight,
            preferred_element_type=jnp.float32,
        )
        * score_scale
    ).astype(jnp.bfloat16)
    seq_rows = queries.shape[0]
    shifted = jnp.concatenate(
        [queries[M - 1 :], jnp.zeros((M - 1, local_width), jnp.bfloat16)], axis=0
    )
    shifted = shifted.reshape(spans, M, local_width)
    owner_list = owners.reshape(-1)
    slot_list = slot_ids.reshape(-1)
    ordinal = jnp.arange(neighbours, dtype=jnp.int32)
    earlier = (owner_list[:, None] == owner_list[None, :]) & (ordinal[None, :] < ordinal[:, None])
    position = owner_list * capacity + jnp.sum(earlier.astype(jnp.int32), axis=1)
    placed = position[None, :] == jnp.arange(dp_count * capacity, dtype=jnp.int32)[:, None]
    slot_table = jnp.sum(jnp.where(placed, slot_list[None, :], 0), axis=1).reshape(
        dp_count, capacity
    )
    incoming = lax.all_to_all(slot_table, "dp", split_axis=0, concat_axis=0, tiled=True)
    flat_slots = incoming.reshape(-1)
    sent_keys = jnp.take(key_cache, flat_slots, axis=0).reshape(dp_count, capacity, NL, local_width)
    sent_values = jnp.take(value_cache, flat_slots, axis=0).reshape(
        dp_count, capacity, NL, local_width
    )
    got_keys, got_values = (
        lax.all_to_all(sent_keys, "dp", split_axis=0, concat_axis=0, tiled=True),
        lax.all_to_all(sent_values, "dp", split_axis=0, concat_axis=0, tiled=True),
    )
    key_blocks = jnp.take(got_keys.reshape(dp_count * capacity, NL, local_width), position, axis=0)
    value_blocks = jnp.take(
        got_values.reshape(dp_count * capacity, NL, local_width), position, axis=0
    )
    key_blocks = key_blocks.reshape(spans, 2 * NL, local_width)
    value_blocks = value_blocks.reshape(spans, 2 * NL, local_width)
    attended = span_attention(shifted, key_blocks, value_blocks, valid_counts, head_count)
    flat_rows = attended.reshape(seq_rows, local_width)
    attended = jnp.concatenate(
        [jnp.zeros((M - 1, local_width), jnp.bfloat16), flat_rows[: seq_rows - M + 1]], axis=0
    )
    return lax.psum_scatter(
        jnp.dot(attended, output_weight, preferred_element_type=jnp.float32).astype(jnp.bfloat16),
        "mp",
        scatter_dimension=0,
        tiled=True,
    )


SHARD_ORDER = ((3, 2, 1, 0), (3, 2, 0, 1), (0, 1, 3, 2), (0, 1, 2, 3))
QUERY_ARRAY = {0: 0, -1: 1, 1: 2, 2: 3, -2: 3, 3: 4, -3: 4}
OUTWARD = ((1, 0), (2, 3))
INWARD = ((0, 1), (3, 2))
MIDDLE = ((1, 2), (2, 1))


def attention_kernel(step, blocks, steps_ref, relative_ref, slots_ref, counts_ref, *refs):
    query_refs = refs[:5]
    key_refs = refs[5:13]
    value_refs = refs[13:21]
    out_ref = refs[21]
    query_buf, key_buf, value_buf, total_buf, query_sem, cache_sem = refs[22:]
    shard = steps_ref[2 * step]
    query_array = steps_ref[2 * step + 1]
    rows, width = query_buf.shape
    head_count = width // HD

    for index, query_ref in enumerate(query_refs):

        @pl.when(query_array == index)
        def _():
            pltpu.make_async_copy(query_ref, query_buf, query_sem).start()

    def entry_of(turn):
        span = shard * blocks - 1 + turn
        index = jnp.maximum(span, 0)
        return index, jnp.where(span < 0, 0, counts_ref[index])

    def copies(turn, neighbour, slot, index):
        for kind, (source, buf) in enumerate(((key_refs, key_buf), (value_refs, value_buf))):
            yield pltpu.make_async_copy(
                source[index].at[slot],
                buf.at[turn, pl.ds(neighbour * NL, NL)],
                cache_sem.at[turn, 2 * neighbour + kind],
            )

    def fetch(turn, carry):
        entry, count = entry_of(turn)

        @pl.when(count > 0)
        def _():
            for neighbour in range(2):
                relative = relative_ref[entry * 2 + neighbour]
                slot = slots_ref[entry * 2 + neighbour]
                for index in range(8):

                    @pl.when(relative == index)
                    def _():
                        for copy in copies(turn, neighbour, slot, index):
                            copy.start()

        return carry

    lax.fori_loop(0, blocks + 1, fetch, 0)
    pltpu.make_async_copy(query_refs[0], query_buf, query_sem).wait()

    def attend(turn, carry):
        _, count = entry_of(turn)
        start = pl.multiple_of(jnp.minimum(turn, blocks - 1) * M, M)
        before_start = pl.multiple_of(jnp.maximum(turn - 1, 0) * M, M)
        earlier = pl.ds(pl.multiple_of(before_start + M - 8, 8), 8)

        @pl.when(count > 0)
        def _():
            for neighbour in range(2):
                for copy in copies(turn, neighbour, 0, 0):
                    copy.wait()
            real = lax.broadcasted_iota(jnp.int32, (M, 2 * NL), 1) < count * NL
            row = lax.broadcasted_iota(jnp.int32, (M, HD), 0)
            for head in range(head_count):
                columns = pl.ds(head * HD, HD)
                queries = query_buf[pl.ds(start, M), columns].astype(jnp.float32)
                before = query_buf[pl.ds(before_start, M), columns].astype(jnp.float32)
                queries = jnp.where(row == M - 1, before, queries).astype(jnp.bfloat16)
                scores = lax.dot_general(
                    queries,
                    key_buf[turn, :, columns],
                    (((1,), (1,)), ((), ())),
                    preferred_element_type=jnp.float32,
                )
                scores = jnp.where(real, scores, -1e30)
                weights = jnp.exp(scores - jnp.max(scores, axis=-1, keepdims=True))
                totals = jnp.sum(weights, axis=-1, keepdims=True)
                mixture = jnp.dot(
                    weights.astype(jnp.bfloat16),
                    value_buf[turn, :, columns],
                    preferred_element_type=jnp.float32,
                )
                mixture = mixture / totals

                @pl.when(turn < blocks)
                def _():
                    total_buf[pl.ds(start, M), columns] = mixture

                total_buf[earlier, columns] = jnp.where(
                    row[:8] == 7, mixture[M - 8 :], total_buf[earlier, columns]
                )

        @pl.when(count <= 0)
        def _():
            @pl.when(turn < blocks)
            def _():
                total_buf[pl.ds(start, M), :] = jnp.zeros((M, width), jnp.float32)

            row = lax.broadcasted_iota(jnp.int32, (8, width), 0)
            total_buf[earlier, :] = jnp.where(row == 7, 0.0, total_buf[earlier, :])

        return carry

    lax.fori_loop(0, blocks + 1, attend, 0)
    out_ref[...] = total_buf[...].astype(jnp.bfloat16)


def shard_attention(step, steps, relative, slots, counts, queries, keys, values):
    rows, width = queries[0].shape
    blocks = rows // M
    anywhere = pl.BlockSpec(memory_space=pl.ANY)
    return pl.pallas_call(
        functools.partial(attention_kernel, step, blocks),
        out_shape=jax.ShapeDtypeStruct((rows, width), jnp.bfloat16),
        grid_spec=pltpu.PrefetchScalarGridSpec(
            num_scalar_prefetch=4,
            grid=(1,),
            in_specs=[anywhere] * 21,
            out_specs=pl.BlockSpec((rows, width), lambda i, *_: (0, 0)),
            scratch_shapes=[
                pltpu.VMEM((rows, width), jnp.bfloat16),
                pltpu.VMEM((blocks + 1, 2 * NL, width), jnp.bfloat16),
                pltpu.VMEM((blocks + 1, 2 * NL, width), jnp.bfloat16),
                pltpu.VMEM((rows, width), jnp.float32),
                pltpu.SemaphoreType.DMA,
                pltpu.SemaphoreType.DMA((blocks + 1, 4)),
            ],
        ),
        compiler_params=pltpu.CompilerParams(vmem_limit_bytes=24 << 20),
        cost_estimate=pl.CostEstimate(
            flops=4 * rows * 2 * NL * width,
            bytes_accessed=2 * (rows * width * 2 + (blocks + 1) * 2 * NL * width * 2),
            transcendentals=rows * 2 * NL * (width // HD),
        ),
    )(steps, relative, slots, counts, *queries, *keys, *values)


def swap(values, bits):
    return lax.ppermute(values, "dp", [(i, i ^ bits) for i in range(8)])


def along(values, pairs):
    return lax.ppermute(values, "mp", list(pairs))


def cube_on_device(
    tokens,
    norm_gain,
    query_weight,
    output_weight,
    key_cache,
    value_cache,
    owners,
    slot_ids,
    valid_counts,
):
    score_scale = 1.0 / math.sqrt(HD)
    place = lax.axis_index("mp")

    def project(rows):
        return (jnp.dot(rows, query_weight, preferred_element_type=jnp.float32) * score_scale).astype(
            jnp.bfloat16
        )

    together = lax.optimization_barrier
    normed = layer_norm(tokens, norm_gain)
    below = along(normed, ((0, 1), (1, 2), (2, 3)))
    above = along(normed, ((1, 0), (2, 1), (3, 2)))
    keys = [key_cache, swap(key_cache, 1), swap(key_cache, 2)] + [None] * 5
    values = [value_cache, swap(value_cache, 1), None, None, swap(value_cache, 4)] + [None] * 3
    below, above, keys[2], values[4], key_cache, value_cache = together(
        (below, above, keys[2], values[4], key_cache, value_cache)
    )
    below_two = along(below, ((1, 2), (2, 3)))
    above_two = along(above, ((1, 0), (2, 1)))
    values[2], keys[4] = swap(value_cache, 2), swap(key_cache, 4)
    keys[3], values[5] = swap(keys[2], 1), swap(values[4], 1)
    below_two, above_two, values[2], keys[4], keys_x, values_y = together(
        (below_two, above_two, values[2], keys[4], keys[2], values[4])
    )
    two = jnp.where(place >= 2, below_two, above_two)
    three = along(two, OUTWARD)
    keys[6], values[6] = swap(keys_x, 4), swap(values_y, 2)
    values[3], keys[5] = swap(values[2], 1), swap(keys[4], 1)
    keys[7], values[7] = swap(keys[6], 1), swap(values[6], 1)
    queries = [project(rows) for rows in (normed, below, above, two, three)]

    table = [
        [number for shard in order for number in (shard, QUERY_ARRAY[shard - z])]
        for z, order in enumerate(SHARD_ORDER)
    ]
    steps = lax.dynamic_index_in_dim(jnp.array(table, jnp.int32), place, 0, keepdims=False)
    relative = owners.reshape(-1) ^ lax.axis_index("dp")
    slots = slot_ids.reshape(-1)

    def part(step):
        attended = shard_attention(step, steps, relative, slots, valid_counts, queries, keys, values)
        return jnp.dot(attended, output_weight, preferred_element_type=jnp.float32).astype(jnp.bfloat16)

    def plus(*terms):
        total = terms[0].astype(jnp.float32)
        for term in terms[1:]:
            total = total + term.astype(jnp.float32)
        return total.astype(jnp.bfloat16)

    first = part(0)
    first_in = along(first, INWARD)
    second = part(1)
    second_in = along(second, INWARD)
    first_middle = along(plus(first, first_in), MIDDLE)
    third = part(2)
    third_in = along(third, INWARD)
    second_middle = along(plus(second, second_in), MIDDLE)
    third_out = along(plus(third, first_middle), OUTWARD)
    own = part(3)
    return plus(own, third_in, second_middle, third_out)


def on_device(*arguments):
    if lax.axis_size("mp") == 4 and lax.axis_size("dp") == 8:
        return cube_on_device(*arguments)
    return general_on_device(*arguments)


def solution(mesh):
    placed = (
        P(("dp", "mp"), None),
        P(),
        P(None, "mp"),
        P("mp", None),
        P("dp", None, "mp"),
        P("dp", None, "mp"),
        P("dp", None),
        P("dp", None),
        P("dp"),
    )
    return jax.shard_map(
        on_device, mesh=mesh, in_specs=placed, out_specs=P(("dp", "mp"), None), check_vma=False
    )
```

```python
import functools
import math

import jax
import jax.numpy as jnp
from jax import lax
from jax.experimental import pallas as pl
from jax.experimental.pallas import tpu as pltpu
from jax.sharding import PartitionSpec as P

HD = 128
M = 64
NL = 128


def layer_norm(token_rows, norm_gain):
    values = token_rows.astype(jnp.float32)
    row_mean = jnp.mean(values, axis=-1, keepdims=True)
    centered = values - row_mean
    variance = jnp.mean(centered * centered, axis=-1, keepdims=True)
    return (centered * lax.rsqrt(variance + 1e-05) * norm_gain).astype(jnp.bfloat16)


def span_attention(queries, key_blocks, value_blocks, valid_counts, head_count):
    spans, length, local_width = queries.shape
    query_heads = queries.reshape(spans, length, head_count, HD)
    key_heads = key_blocks.reshape(spans, -1, head_count, HD)
    value_heads = value_blocks.reshape(spans, -1, head_count, HD)
    scores = jnp.einsum(
        "cmhd,ckhd->chmk", query_heads, key_heads, preferred_element_type=jnp.float32
    )
    usable = (jnp.arange(key_heads.shape[1], dtype=jnp.int32) // NL)[None, :] < valid_counts[
        :, None
    ]
    usable = usable[:, None, None, :]
    masked = jnp.where(usable, scores, -1e30)
    highest = jnp.max(masked, axis=-1, keepdims=True)
    weights = jnp.where(usable, jnp.exp(masked - highest), 0.0)
    totals = jnp.sum(weights, axis=-1) + (valid_counts == 0).astype(jnp.float32)[:, None, None]
    mixture = jnp.einsum(
        "chmk,ckhd->cmhd",
        weights.astype(jnp.bfloat16),
        value_heads,
        preferred_element_type=jnp.float32,
    )
    mixture = mixture / jnp.transpose(totals, (0, 2, 1))[..., None]
    return mixture.reshape(spans, length, local_width).astype(jnp.bfloat16)


def general_on_device(
    tokens,
    norm_gain,
    query_weight,
    output_weight,
    key_cache,
    value_cache,
    owners,
    slot_ids,
    valid_counts,
):
    dp_count = lax.axis_size("dp")
    local_width = query_weight.shape[1]
    head_count = local_width // HD
    spans = valid_counts.shape[0]
    neighbours = 2 * spans
    capacity = max(2, (neighbours + dp_count - 1) // dp_count)
    score_scale = 1.0 / math.sqrt(HD)
    normed = layer_norm(tokens, norm_gain)
    queries = (
        jnp.dot(
            lax.all_gather(normed, "mp", axis=0, tiled=True),
            query_weight,
            preferred_element_type=jnp.float32,
        )
        * score_scale
    ).astype(jnp.bfloat16)
    seq_rows = queries.shape[0]
    shifted = jnp.concatenate(
        [queries[M - 1 :], jnp.zeros((M - 1, local_width), jnp.bfloat16)], axis=0
    )
    shifted = shifted.reshape(spans, M, local_width)
    owner_list = owners.reshape(-1)
    slot_list = slot_ids.reshape(-1)
    ordinal = jnp.arange(neighbours, dtype=jnp.int32)
    earlier = (owner_list[:, None] == owner_list[None, :]) & (ordinal[None, :] < ordinal[:, None])
    position = owner_list * capacity + jnp.sum(earlier.astype(jnp.int32), axis=1)
    placed = position[None, :] == jnp.arange(dp_count * capacity, dtype=jnp.int32)[:, None]
    slot_table = jnp.sum(jnp.where(placed, slot_list[None, :], 0), axis=1).reshape(
        dp_count, capacity
    )
    incoming = lax.all_to_all(slot_table, "dp", split_axis=0, concat_axis=0, tiled=True)
    flat_slots = incoming.reshape(-1)
    sent_keys = jnp.take(key_cache, flat_slots, axis=0).reshape(dp_count, capacity, NL, local_width)
    sent_values = jnp.take(value_cache, flat_slots, axis=0).reshape(
        dp_count, capacity, NL, local_width
    )
    got_keys, got_values = (
        lax.all_to_all(sent_keys, "dp", split_axis=0, concat_axis=0, tiled=True),
        lax.all_to_all(sent_values, "dp", split_axis=0, concat_axis=0, tiled=True),
    )
    key_blocks = jnp.take(got_keys.reshape(dp_count * capacity, NL, local_width), position, axis=0)
    value_blocks = jnp.take(
        got_values.reshape(dp_count * capacity, NL, local_width), position, axis=0
    )
    key_blocks = key_blocks.reshape(spans, 2 * NL, local_width)
    value_blocks = value_blocks.reshape(spans, 2 * NL, local_width)
    attended = span_attention(shifted, key_blocks, value_blocks, valid_counts, head_count)
    flat_rows = attended.reshape(seq_rows, local_width)
    attended = jnp.concatenate(
        [jnp.zeros((M - 1, local_width), jnp.bfloat16), flat_rows[: seq_rows - M + 1]], axis=0
    )
    return lax.psum_scatter(
        jnp.dot(attended, output_weight, preferred_element_type=jnp.float32).astype(jnp.bfloat16),
        "mp",
        scatter_dimension=0,
        tiled=True,
    )


SHARD_ORDER = ((3, 2, 1, 0), (3, 2, 1, 0), (0, 1, 2, 3), (0, 1, 2, 3))
HEADS_TOGETHER = 8
OUTWARD = ((1, 0), (2, 3))
INWARD = ((0, 1), (3, 2))
MIDDLE = ((1, 2), (2, 1))


def attention_kernel(step, blocks, order_ref, relative_ref, slots_ref, counts_ref, *refs):
    query_buf = refs[0]
    pair_refs = refs[1:7]
    key_refs = [ref.at[0] for ref in pair_refs] + [refs[7], refs[9]]
    value_refs = [ref.at[1] for ref in pair_refs] + [refs[8], refs[10]]
    out_ref = refs[11]
    key_buf, value_buf, total_buf, cache_sem = refs[12:]
    shard = order_ref[step]
    rows, width = query_buf.shape
    head_count = width // HD

    def entry_of(turn):
        span = shard * blocks - 1 + turn
        index = jnp.maximum(span, 0)
        return index, jnp.where(span < 0, 0, counts_ref[index])

    def copies(turn, neighbour, slot, index):
        for kind, (source, buf) in enumerate(((key_refs, key_buf), (value_refs, value_buf))):
            yield pltpu.make_async_copy(
                source[index].at[slot],
                buf.at[turn, pl.ds(neighbour * NL, NL)],
                cache_sem.at[turn, 2 * neighbour + kind],
            )

    def fetch(turn, carry):
        entry, count = entry_of(turn)

        @pl.when(count > 0)
        def _():
            for neighbour in range(2):
                relative = relative_ref[entry * 2 + neighbour]
                slot = slots_ref[entry * 2 + neighbour]
                for index in range(8):

                    @pl.when(relative == index)
                    def _():
                        for copy in copies(turn, neighbour, slot, index):
                            copy.start()

        return carry

    lax.fori_loop(0, blocks + 1, fetch, 0)

    def attend(turn, carry):
        _, count = entry_of(turn)
        start = pl.multiple_of(turn * M, M)
        block = pl.ds(pl.multiple_of(jnp.minimum(turn, blocks - 1) * M, M), M)
        before = pl.ds(pl.multiple_of(jnp.maximum(turn - 1, 0) * M + M - 16, 16), 16)
        earlier = pl.ds(pl.multiple_of(jnp.maximum(turn - 1, 0) * M + M - 8, 8), 8)

        @pl.when(count > 0)
        def _():
            for neighbour in range(2):
                for copy in copies(turn, neighbour, 0, 0):
                    copy.wait()
            real = lax.broadcasted_iota(jnp.int32, (M, 2 * NL), 1) < count * NL
            row = lax.broadcasted_iota(jnp.int32, (16, HD), 0)
            for first_head in range(0, head_count, HEADS_TOGETHER):
                heads = [
                    pl.ds(head * HD, HD) for head in range(first_head, first_head + HEADS_TOGETHER)
                ]
                weights = []
                for columns in heads:
                    queries = query_buf[block, columns]
                    tail = jnp.where(
                        row == 15,
                        query_buf[before, columns].astype(jnp.float32),
                        queries[M - 16 :].astype(jnp.float32),
                    ).astype(jnp.bfloat16)
                    scores = lax.dot_general(
                        jnp.concatenate([queries[: M - 16], tail], axis=0),
                        key_buf[turn, :, columns],
                        (((1,), (1,)), ((), ())),
                        preferred_element_type=jnp.float32,
                    )
                    weights.append(jnp.where(real, scores, -1e30))
                weights = [jnp.exp(w - jnp.max(w, axis=-1, keepdims=True)) for w in weights]
                shares = [1.0 / jnp.sum(w, axis=-1, keepdims=True) for w in weights]
                for columns, weight, share in zip(heads, weights, shares):
                    mixture = share * jnp.dot(
                        weight.astype(jnp.bfloat16),
                        value_buf[turn, :, columns],
                        preferred_element_type=jnp.float32,
                    )
                    total_buf[pl.ds(start, M), columns] = mixture
                    total_buf[earlier, columns] = jnp.where(
                        row[8:] == 15, mixture[M - 8 :], total_buf[earlier, columns]
                    )

        @pl.when(count <= 0)
        def _():
            total_buf[pl.ds(start, M), :] = jnp.zeros((M, width), jnp.float32)
            row = lax.broadcasted_iota(jnp.int32, (8, width), 0)
            total_buf[earlier, :] = jnp.where(row == 7, 0.0, total_buf[earlier, :])

        return carry

    lax.fori_loop(0, blocks + 1, attend, 0)
    out_ref[...] = total_buf[:rows].astype(jnp.bfloat16)


def shard_attention(step, order, relative, slots, counts, queries, caches):
    rows, width = queries.shape
    blocks = rows // M
    anywhere = pl.BlockSpec(memory_space=pl.ANY)
    return pl.pallas_call(
        functools.partial(attention_kernel, step, blocks),
        out_shape=jax.ShapeDtypeStruct((rows, width), jnp.bfloat16),
        grid_spec=pltpu.PrefetchScalarGridSpec(
            num_scalar_prefetch=4,
            grid=(1,),
            in_specs=[pl.BlockSpec((rows, width), lambda i, *_: (0, 0))] + [anywhere] * 10,
            out_specs=pl.BlockSpec((rows, width), lambda i, *_: (0, 0)),
            scratch_shapes=[
                pltpu.VMEM((blocks + 1, 2 * NL, width), jnp.bfloat16),
                pltpu.VMEM((blocks + 1, 2 * NL, width), jnp.bfloat16),
                pltpu.VMEM((rows + M, width), jnp.float32),
                pltpu.SemaphoreType.DMA((blocks + 1, 4)),
            ],
        ),
        compiler_params=pltpu.CompilerParams(vmem_limit_bytes=16 << 20),
        cost_estimate=pl.CostEstimate(
            flops=4 * rows * 2 * NL * width,
            bytes_accessed=2 * (rows * width * 2 + (blocks + 1) * 2 * NL * width * 2),
            transcendentals=rows * 2 * NL * (width // HD),
        ),
    )(order, relative, slots, counts, queries, *caches)


def swap(values, bits):
    return lax.ppermute(values, "dp", [(i, i ^ bits) for i in range(8)])


def along(values, pairs):
    return lax.ppermute(values, "mp", list(pairs))


def cube_on_device(
    tokens,
    norm_gain,
    query_weight,
    output_weight,
    key_cache,
    value_cache,
    owners,
    slot_ids,
    valid_counts,
):
    score_scale = 1.0 / math.sqrt(HD)
    place = lax.axis_index("mp")

    def project(rows):
        return (jnp.dot(rows, query_weight, preferred_element_type=jnp.float32) * score_scale).astype(
            jnp.bfloat16
        )

    together = lax.optimization_barrier
    core = lax.axis_index("dp") % 2
    half = output_weight.shape[0] // 2
    inside = (place == 1) | (place == 2)
    low = place < 2
    normed = layer_norm(tokens, norm_gain)
    below = along(normed, ((0, 1), (1, 2), (2, 3)))
    above = along(normed, ((1, 0), (2, 1), (3, 2)))
    cache = jnp.stack([key_cache, value_cache])
    cache_x, cache_y, cache_core = swap(cache, 2), swap(cache, 4), swap(cache, 1)
    handed = lax.dynamic_slice_in_dim(output_weight, core * half, half, 0)
    below, above, handed = together((below, above, handed))
    below_two = along(below, ((1, 2), (2, 3)))
    above_two = along(above, ((1, 0), (2, 1)))
    inner = along(handed, INWARD)
    third_queries = project(jnp.where(inside, normed, jnp.where(low, above, below)))
    fourth_queries = project(jnp.where(inside, jnp.where(low, below, above), normed))
    below_two, above_two, cache_x, cache_y, third_queries, fourth_queries = together(
        (below_two, above_two, cache_x, cache_y, third_queries, fourth_queries)
    )
    two = jnp.where(low, above_two, below_two)
    three = along(two, OUTWARD)
    keys_xy, values_xy = swap(cache_x[0], 4), swap(cache_y[1], 2)
    cache_x_core, cache_y_core = swap(cache_x, 1), swap(cache_y, 1)
    three, keys_xy, values_xy, inner = together((three, keys_xy, values_xy, inner))
    keys_xy_core, values_xy_core = swap(keys_xy, 1), swap(values_xy, 1)
    other_inner = swap(inner, 1)
    first_queries = project(jnp.where(inside, two, three))
    caches = [cache, cache_core, cache_x, cache_x_core, cache_y, cache_y_core]
    caches += [keys_xy, values_xy, keys_xy_core, values_xy_core]

    order = lax.dynamic_index_in_dim(jnp.array(SHARD_ORDER, jnp.int32), place, 0, keepdims=False)
    relative = owners.reshape(-1) ^ lax.axis_index("dp")
    slots = slot_ids.reshape(-1)

    def attend(step, queries):
        return shard_attention(step, order, relative, slots, valid_counts, queries, caches)

    def product(attended, weight):
        return jnp.dot(attended, weight, preferred_element_type=jnp.float32)

    def handed_product(attended, columns):
        total = None
        for piece, from_core in ((inner, core), (other_inner, 1 - core)):
            heads = lax.dynamic_slice_in_dim(attended, from_core * half, half, 1)
            term = product(heads, piece[:, columns])
            total = term if total is None else total + term
        return total

    def rounded_sum(one, other):
        return (one.astype(jnp.float32) + other.astype(jnp.float32)).astype(jnp.bfloat16)

    width = output_weight.shape[1] // 2
    left, right = slice(0, width), slice(width, 2 * width)
    first = attend(0, first_queries)
    first_in = along(first, INWARD)
    first, two, above, below = together((first, two, above, below))
    first_part = product(first, output_weight)
    second = attend(
        1, project(jnp.where(inside, jnp.where(low, above, below), two))
    )
    second_in = along(second, INWARD)
    first_in, first_part, second = together((first_in, first_part, second))
    first_across = []
    for columns in (left, right):
        piece = rounded_sum(first_part[:, columns], handed_product(first_in, columns))
        piece, fourth_queries, second, first_in = together((piece, fourth_queries, second, first_in))
        first_across.append(along(piece, MIDDLE))
    fourth = product(attend(3, fourth_queries), output_weight).astype(jnp.bfloat16)
    second_part = product(second, output_weight)
    first_left, fourth, second_part, second_in = together((first_across[0], fourth, second_part, second_in))
    outward_left = along(rounded_sum(fourth[:, left], first_left), OUTWARD)
    second = rounded_sum(second_part, handed_product(second_in, slice(0, 2 * width)))
    second, third_queries = together((second, third_queries))
    second_across = along(second, MIDDLE)
    outward_right = along(rounded_sum(fourth[:, right], first_across[1]), OUTWARD)
    third = attend(2, third_queries)
    third_in = along(third, INWARD)
    third = rounded_sum(product(third, output_weight), handed_product(third_in, slice(0, 2 * width)))
    third, fourth, second_across, outward_left, outward_right = together(
        (third, fourth, second_across, outward_left, outward_right)
    )
    return rounded_sum(
        jnp.where(inside, third, fourth),
        jnp.where(inside, second_across, jnp.concatenate([outward_left, outward_right], axis=1)),
    )


def on_device(*arguments):
    if lax.axis_size("mp") == 4 and lax.axis_size("dp") == 8:
        return cube_on_device(*arguments)
    return general_on_device(*arguments)


def solution(mesh):
    placed = (
        P(("dp", "mp"), None),
        P(),
        P(None, "mp"),
        P("mp", None),
        P("dp", None, "mp"),
        P("dp", None, "mp"),
        P("dp", None),
        P("dp", None),
        P("dp"),
    )
    return jax.shard_map(
        on_device, mesh=mesh, in_specs=placed, out_specs=P(("dp", "mp"), None), check_vma=False
    )
```

```python
import functools
import math

import jax
import jax.numpy as jnp
from jax import lax
from jax.experimental import pallas as pl
from jax.experimental.pallas import tpu as pltpu
from jax.sharding import PartitionSpec as P

HD = 128
M = 64
NL = 128


def layer_norm(token_rows, norm_gain):
    values = token_rows.astype(jnp.float32)
    row_mean = jnp.mean(values, axis=-1, keepdims=True)
    centered = values - row_mean
    variance = jnp.mean(centered * centered, axis=-1, keepdims=True)
    return (centered * lax.rsqrt(variance + 1e-05) * norm_gain).astype(jnp.bfloat16)


def span_attention(queries, key_blocks, value_blocks, valid_counts, head_count):
    spans, length, local_width = queries.shape
    query_heads = queries.reshape(spans, length, head_count, HD)
    key_heads = key_blocks.reshape(spans, -1, head_count, HD)
    value_heads = value_blocks.reshape(spans, -1, head_count, HD)
    scores = jnp.einsum(
        "cmhd,ckhd->chmk", query_heads, key_heads, preferred_element_type=jnp.float32
    )
    usable = (jnp.arange(key_heads.shape[1], dtype=jnp.int32) // NL)[None, :] < valid_counts[
        :, None
    ]
    usable = usable[:, None, None, :]
    masked = jnp.where(usable, scores, -1e30)
    highest = jnp.max(masked, axis=-1, keepdims=True)
    weights = jnp.where(usable, jnp.exp(masked - highest), 0.0)
    totals = jnp.sum(weights, axis=-1) + (valid_counts == 0).astype(jnp.float32)[:, None, None]
    mixture = jnp.einsum(
        "chmk,ckhd->cmhd",
        weights.astype(jnp.bfloat16),
        value_heads,
        preferred_element_type=jnp.float32,
    )
    mixture = mixture / jnp.transpose(totals, (0, 2, 1))[..., None]
    return mixture.reshape(spans, length, local_width).astype(jnp.bfloat16)


def general_on_device(
    tokens,
    norm_gain,
    query_weight,
    output_weight,
    key_cache,
    value_cache,
    owners,
    slot_ids,
    valid_counts,
):
    dp_count = lax.axis_size("dp")
    local_width = query_weight.shape[1]
    head_count = local_width // HD
    spans = valid_counts.shape[0]
    neighbours = 2 * spans
    capacity = max(2, (neighbours + dp_count - 1) // dp_count)
    score_scale = 1.0 / math.sqrt(HD)
    normed = layer_norm(tokens, norm_gain)
    queries = (
        jnp.dot(
            lax.all_gather(normed, "mp", axis=0, tiled=True),
            query_weight,
            preferred_element_type=jnp.float32,
        )
        * score_scale
    ).astype(jnp.bfloat16)
    seq_rows = queries.shape[0]
    shifted = jnp.concatenate(
        [queries[M - 1 :], jnp.zeros((M - 1, local_width), jnp.bfloat16)], axis=0
    )
    shifted = shifted.reshape(spans, M, local_width)
    owner_list = owners.reshape(-1)
    slot_list = slot_ids.reshape(-1)
    ordinal = jnp.arange(neighbours, dtype=jnp.int32)
    earlier = (owner_list[:, None] == owner_list[None, :]) & (ordinal[None, :] < ordinal[:, None])
    position = owner_list * capacity + jnp.sum(earlier.astype(jnp.int32), axis=1)
    placed = position[None, :] == jnp.arange(dp_count * capacity, dtype=jnp.int32)[:, None]
    slot_table = jnp.sum(jnp.where(placed, slot_list[None, :], 0), axis=1).reshape(
        dp_count, capacity
    )
    incoming = lax.all_to_all(slot_table, "dp", split_axis=0, concat_axis=0, tiled=True)
    flat_slots = incoming.reshape(-1)
    sent_keys = jnp.take(key_cache, flat_slots, axis=0).reshape(dp_count, capacity, NL, local_width)
    sent_values = jnp.take(value_cache, flat_slots, axis=0).reshape(
        dp_count, capacity, NL, local_width
    )
    got_keys, got_values = (
        lax.all_to_all(sent_keys, "dp", split_axis=0, concat_axis=0, tiled=True),
        lax.all_to_all(sent_values, "dp", split_axis=0, concat_axis=0, tiled=True),
    )
    key_blocks = jnp.take(got_keys.reshape(dp_count * capacity, NL, local_width), position, axis=0)
    value_blocks = jnp.take(
        got_values.reshape(dp_count * capacity, NL, local_width), position, axis=0
    )
    key_blocks = key_blocks.reshape(spans, 2 * NL, local_width)
    value_blocks = value_blocks.reshape(spans, 2 * NL, local_width)
    attended = span_attention(shifted, key_blocks, value_blocks, valid_counts, head_count)
    flat_rows = attended.reshape(seq_rows, local_width)
    attended = jnp.concatenate(
        [jnp.zeros((M - 1, local_width), jnp.bfloat16), flat_rows[: seq_rows - M + 1]], axis=0
    )
    return lax.psum_scatter(
        jnp.dot(attended, output_weight, preferred_element_type=jnp.float32).astype(jnp.bfloat16),
        "mp",
        scatter_dimension=0,
        tiled=True,
    )


SHARD_ORDER = ((3, 2, 1, 0), (3, 2, 1, 0), (0, 1, 2, 3), (0, 1, 2, 3))
HEADS_TOGETHER = 8
SMALL = pl.CostEstimate(flops=1, bytes_accessed=1, transcendentals=0)
OUTWARD = ((1, 0), (2, 3))
INWARD = ((0, 1), (3, 2))
MIDDLE = ((1, 2), (2, 1))


def in_hbm(values):
    return pltpu.with_memory_space_constraint(values, pltpu.HBM)


def attention_kernel(step, blocks, order_ref, relative_ref, slots_ref, counts_ref, *refs):
    query_buf = refs[0]
    key_refs = refs[1:9]
    value_refs = refs[9:17]
    out_ref = refs[17]
    key_buf, value_buf, total_buf, cache_sem = refs[18:]
    shard = order_ref[step]
    rows, width = query_buf.shape
    head_count = width // HD

    def entry_of(turn):
        span = shard * blocks - 1 + turn
        index = jnp.maximum(span, 0)
        return index, jnp.where(span < 0, 0, counts_ref[index])

    def copies(turn, neighbour, slot, index):
        for kind, (source, buf) in enumerate(((key_refs, key_buf), (value_refs, value_buf))):
            yield pltpu.make_async_copy(
                source[index].at[slot],
                buf.at[turn, pl.ds(neighbour * NL, NL)],
                cache_sem.at[turn, 2 * neighbour + kind],
            )

    def fetch(turn, carry):
        entry, count = entry_of(turn)

        @pl.when(count > 0)
        def _():
            for neighbour in range(2):
                relative = relative_ref[entry * 2 + neighbour]
                slot = slots_ref[entry * 2 + neighbour]
                for index in range(8):

                    @pl.when(relative == index)
                    def _():
                        for copy in copies(turn, neighbour, slot, index):
                            copy.start()

        return carry

    lax.fori_loop(0, blocks + 1, fetch, 0)

    def attend(turn, carry):
        _, count = entry_of(turn)
        start = pl.multiple_of(turn * M, M)
        block = pl.ds(pl.multiple_of(jnp.minimum(turn, blocks - 1) * M, M), M)
        before = pl.ds(pl.multiple_of(jnp.maximum(turn - 1, 0) * M + M - 16, 16), 16)
        earlier = pl.ds(pl.multiple_of(jnp.maximum(turn - 1, 0) * M + M - 8, 8), 8)

        @pl.when(count > 0)
        def _():
            for neighbour in range(2):
                for copy in copies(turn, neighbour, 0, 0):
                    copy.wait()
            real = lax.broadcasted_iota(jnp.int32, (M, 2 * NL), 1) < count * NL
            row = lax.broadcasted_iota(jnp.int32, (16, HD), 0)
            for first_head in range(0, head_count, HEADS_TOGETHER):
                heads = [
                    pl.ds(head * HD, HD) for head in range(first_head, first_head + HEADS_TOGETHER)
                ]
                weights = []
                for columns in heads:
                    queries = query_buf[block, columns]
                    tail = jnp.where(
                        row == 15,
                        query_buf[before, columns].astype(jnp.float32),
                        queries[M - 16 :].astype(jnp.float32),
                    ).astype(jnp.bfloat16)
                    scores = lax.dot_general(
                        jnp.concatenate([queries[: M - 16], tail], axis=0),
                        key_buf[turn, :, columns],
                        (((1,), (1,)), ((), ())),
                        preferred_element_type=jnp.float32,
                    )
                    weights.append(jnp.where(real, scores, -1e30))
                weights = [jnp.exp(w - jnp.max(w, axis=-1, keepdims=True)) for w in weights]
                shares = [1.0 / jnp.sum(w, axis=-1, keepdims=True) for w in weights]
                for columns, weight, share in zip(heads, weights, shares):
                    mixture = share * jnp.dot(
                        weight.astype(jnp.bfloat16),
                        value_buf[turn, :, columns],
                        preferred_element_type=jnp.float32,
                    )
                    total_buf[pl.ds(start, M), columns] = mixture
                    total_buf[earlier, columns] = jnp.where(
                        row[8:] == 15, mixture[M - 8 :], total_buf[earlier, columns]
                    )

        @pl.when(count <= 0)
        def _():
            total_buf[pl.ds(start, M), :] = jnp.zeros((M, width), jnp.float32)
            row = lax.broadcasted_iota(jnp.int32, (8, width), 0)
            total_buf[earlier, :] = jnp.where(row == 7, 0.0, total_buf[earlier, :])

        return carry

    lax.fori_loop(0, blocks + 1, attend, 0)
    out_ref[...] = total_buf[:rows].astype(jnp.bfloat16)


def shard_attention(step, order, relative, slots, counts, queries, keys, values):
    rows, width = queries.shape
    blocks = rows // M
    anywhere = pl.BlockSpec(memory_space=pltpu.HBM)
    return pl.pallas_call(
        functools.partial(attention_kernel, step, blocks),
        out_shape=jax.ShapeDtypeStruct((rows, width), jnp.bfloat16),
        grid_spec=pltpu.PrefetchScalarGridSpec(
            num_scalar_prefetch=4,
            grid=(1,),
            in_specs=[pl.BlockSpec((rows, width), lambda i, *_: (0, 0))] + [anywhere] * 16,
            out_specs=pl.BlockSpec((rows, width), lambda i, *_: (0, 0)),
            scratch_shapes=[
                pltpu.VMEM((blocks + 1, 2 * NL, width), jnp.bfloat16),
                pltpu.VMEM((blocks + 1, 2 * NL, width), jnp.bfloat16),
                pltpu.VMEM((rows + M, width), jnp.float32),
                pltpu.SemaphoreType.DMA((blocks + 1, 4)),
            ],
        ),
        compiler_params=pltpu.CompilerParams(vmem_limit_bytes=16 << 20),
        cost_estimate=SMALL,
    )(order, relative, slots, counts, queries, *keys, *values)


def project_kernel(scale, which_ref, *refs):
    sources = refs[: len(refs) - 4]
    weight_ref, out_ref, rows_buf, sem = refs[len(refs) - 4 :]

    @pl.when(pl.program_id(0) == 0)
    def _():
        for index, source in enumerate(sources):

            @pl.when(which_ref[0] == index)
            def _():
                copy = pltpu.make_async_copy(source, rows_buf, sem)
                copy.start()
                copy.wait()

    total = jnp.dot(rows_buf[...], weight_ref[...], preferred_element_type=jnp.float32)
    out_ref[...] = (total * scale).astype(jnp.bfloat16)


def project(which, sources, weight, streamed=True):
    rows, depth = sources[0].shape
    width = weight.shape[1]
    return pl.pallas_call(
        functools.partial(project_kernel, 1.0 / math.sqrt(HD)),
        out_shape=jax.ShapeDtypeStruct((rows, width), jnp.bfloat16),
        grid_spec=pltpu.PrefetchScalarGridSpec(
            num_scalar_prefetch=1,
            grid=(width // 256,),
            in_specs=[pl.BlockSpec(memory_space=pltpu.HBM)] * len(sources)
            + [pl.BlockSpec((depth, 256), lambda i, _: (0, i))],
            out_specs=pl.BlockSpec((rows, 256), lambda i, _: (0, i)),
            scratch_shapes=[pltpu.VMEM((rows, depth), jnp.bfloat16), pltpu.SemaphoreType.DMA],
        ),
        compiler_params=pltpu.CompilerParams(vmem_limit_bytes=16 << 20),
        cost_estimate=SMALL,
    )(which.reshape(1), *sources, in_hbm(weight) if streamed else weight)


def output_kernel(core_ref, attended_ref, handed_ref, weight_ref, *refs):
    out_ref = refs[4]
    height = refs[0].shape[0]
    if weight_ref is None:
        total = attended_ref[...]
    else:
        total = jnp.dot(attended_ref[...], weight_ref[...], preferred_element_type=jnp.float32)
    for index, piece in enumerate(refs[:4]):
        from_core = core_ref[0] if index < 2 else 1 - core_ref[0]
        start = from_core * 2 * height + index % 2 * height
        heads = handed_ref[:, pl.ds(pl.multiple_of(start, height), height)]
        total += jnp.dot(heads, piece[...], preferred_element_type=jnp.float32)
    out_ref[...] = total.astype(jnp.bfloat16)


def output_rest_kernel(core_ref, part_ref, handed_ref, *refs):
    output_kernel(core_ref, part_ref, handed_ref, None, *refs)


def output_plus_kernel(attended_ref, weight_ref, plus_ref, out_ref):
    total = jnp.dot(attended_ref[...], weight_ref[...], preferred_element_type=jnp.float32)
    out_ref[...] = (total + plus_ref[...].astype(jnp.float32)).astype(jnp.bfloat16)


def output_only_kernel(attended_ref, weight_ref, out_ref):
    out_ref[...] = jnp.dot(attended_ref[...], weight_ref[...], preferred_element_type=jnp.float32)


def fixed_block(rows, depth):
    return pl.BlockSpec((rows, depth), lambda i, *_: (0, 0))


def column_block(height, start):
    return pl.BlockSpec((height, 512), lambda i, *_: (0, start + i))


def output_call(kernel, prefetched, in_specs, rows, count, kind, *operands):
    return pl.pallas_call(
        kernel,
        out_shape=jax.ShapeDtypeStruct((rows, count * 512), kind),
        grid_spec=pltpu.PrefetchScalarGridSpec(
            num_scalar_prefetch=prefetched,
            grid=(count,),
            in_specs=in_specs,
            out_specs=column_block(rows, 0),
        ),
        compiler_params=pltpu.CompilerParams(vmem_limit_bytes=16 << 20),
        cost_estimate=SMALL,
    )(*operands)


def output_part(core, attended, handed, weight, inner, first, count):
    rows, depth = handed.shape
    inner = [in_hbm(piece) for piece in inner]
    pieces = [column_block(piece.shape[0], first) for piece in inner]
    return output_call(
        output_kernel,
        1,
        [fixed_block(rows, depth), fixed_block(rows, depth), column_block(depth, first)] + pieces,
        rows,
        count,
        jnp.bfloat16,
        core.reshape(1),
        attended,
        handed,
        in_hbm(weight),
        *inner,
    )


def output_rest(core, part, handed, inner, first, count):
    rows, depth = handed.shape
    inner = [in_hbm(piece) for piece in inner]
    pieces = [column_block(piece.shape[0], first) for piece in inner]
    return output_call(
        output_rest_kernel,
        1,
        [column_block(rows, 0), fixed_block(rows, depth)] + pieces,
        rows,
        count,
        jnp.bfloat16,
        core.reshape(1),
        part,
        handed,
        *inner,
    )


def output_only(attended, weight, first, count):
    rows, depth = attended.shape
    return output_call(
        output_only_kernel,
        0,
        [fixed_block(rows, depth), column_block(depth, first)],
        rows,
        count,
        jnp.float32,
        attended,
        in_hbm(weight),
    )


def output_plus(attended, weight, plus, first, count):
    rows, depth = attended.shape
    return output_call(
        output_plus_kernel,
        0,
        [fixed_block(rows, depth), column_block(depth, first), column_block(rows, 0)],
        rows,
        count,
        jnp.bfloat16,
        attended,
        in_hbm(weight),
        plus,
    )


def swap(values, bits):
    return lax.ppermute(values, "dp", [(i, i ^ bits) for i in range(8)])


def along(values, pairs):
    return lax.ppermute(values, "mp", list(pairs))


def cube_on_device(
    tokens,
    norm_gain,
    query_weight,
    output_weight,
    key_cache,
    value_cache,
    owners,
    slot_ids,
    valid_counts,
):
    place = lax.axis_index("mp")

    together = lax.optimization_barrier
    core = lax.axis_index("dp") % 2
    half = output_weight.shape[0] // 2
    inside = (place == 1) | (place == 2)
    keys, values = [key_cache] + [None] * 7, [value_cache] + [None] * 7
    normed = layer_norm(tokens, norm_gain)
    beside = along(normed, INWARD + OUTWARD)
    middle = along(normed, MIDDLE)
    keys_x, values_y = swap(key_cache, 2), swap(value_cache, 4)
    keys[1] = swap(key_cache, 1)
    keys[1], value_source = together((keys[1], value_cache))
    values[1] = swap(value_source, 1)
    handed = [
        lax.dynamic_slice_in_dim(output_weight, core * half + start, half // 2, 0) for start in (0, half // 2)
    ]
    order, third_from, fourth_from, second_from, first_from = (
        lax.dynamic_index_in_dim(jnp.array(table, jnp.int32), place, 0, keepdims=False)
        for table in (SHARD_ORDER, (1, 0, 0, 1), (0, 1, 1, 0), (0, 1, 1, 0), (1, 0, 0, 1))
    )
    relative = owners.reshape(-1) ^ lax.axis_index("dp")
    slots = slot_ids.reshape(-1)
    beside, middle, handed, keys[1], values[1], order, relative, slots, keys_x, values_y, keys_far, values_far = (
        together(
            (
                beside,
                middle,
                handed,
                keys[1],
                values[1],
                order,
                relative,
                slots,
                keys_x,
                values_y,
                key_cache,
                value_cache,
            )
        )
    )
    beside_two = along(beside, MIDDLE)
    middle_two = along(middle, OUTWARD)
    keys_y, values_x = swap(keys_far, 4), swap(values_far, 2)
    inner = [along(handed[0], INWARD)]
    third_queries = project(third_from, (normed, beside), query_weight)
    fourth_queries = project(fourth_from, (normed, beside), query_weight)
    beside_two, middle_two, keys_y, values_x, keys_x, values_y, third_queries, fourth_queries, handed, inner = (
        together(
            (
                beside_two,
                middle_two,
                keys_y,
                values_x,
                keys_x,
                values_y,
                third_queries,
                fourth_queries,
                handed,
                inner,
            )
        )
    )
    keys[2], values[4], keys[4], values[2] = keys_x, values_y, keys_y, values_x
    three = along(beside_two, OUTWARD)
    keys[6], values[6] = swap(keys_x, 4), swap(values_y, 2)
    inner += [along(handed[1], INWARD)]
    second_queries = project(second_from, (middle_two, middle), query_weight)
    keys[3], values[5] = swap(keys_x, 1), swap(values_y, 1)
    keys[3], keys_y, values_x, second_queries = together((keys[3], keys_y, values_x, second_queries))
    keys[5], values[3] = swap(keys_y, 1), swap(values_x, 1)
    three, keys[6], values[6], inner = together((three, keys[6], values[6], inner))
    keys[7], values[7] = swap(keys[6], 1), swap(values[6], 1)
    first_queries = project(first_from, (beside_two, three), query_weight, streamed=False)

    def attend(step, queries):
        return shard_attention(step, order, relative, slots, valid_counts, queries, keys, values)

    def output(attended, handed, first, count):
        return output_part(core, attended, handed, output_weight, inner, first, count)

    tiles = output_weight.shape[1] // 512
    first = attend(0, first_queries)
    first_in = along(first, INWARD)
    first, second_queries, inner = together((first, second_queries, inner))
    inner += [swap(piece, 1) for piece in inner]
    left = output_only(first, output_weight, 0, tiles // 2)
    left, second_queries = together((left, second_queries))
    second = attend(1, second_queries)
    second_in = along(second, INWARD)
    first_in, second = together((first_in, second))
    left = output_rest(core, left, first_in, inner, 0, tiles // 2)
    across_left = along(left, MIDDLE)
    _, first, first_in = together((left, first, first_in))
    right = output(first, first_in, tiles // 2, tiles // 2)
    across_right = along(right, MIDDLE)
    _, fourth_queries = together((right, fourth_queries))
    fourth = attend(3, fourth_queries)
    fourth, third_queries = together((fourth, third_queries))
    third = attend(2, third_queries)
    third_in = along(third, INWARD)
    _, second, second_in = together((third, second, second_in))
    second = output(second, second_in, 0, tiles)
    second_across = along(second, MIDDLE)
    _, fourth, across_left = together((second, fourth, across_left))
    left = output_plus(fourth, output_weight, across_left, 0, tiles // 2)
    outward_left = along(left, OUTWARD)
    fourth, across_right, outward_left, third_in = together((fourth, across_right, outward_left, third_in))
    right = output_plus(fourth, output_weight, across_right, tiles // 2, tiles // 2)
    outward_right = along(right, OUTWARD)
    _, third, third_in = together((right, third, third_in))
    third = output(third, third_in, 0, tiles)
    third, second_across, outward_left, outward_right = together(
        (third, second_across, outward_left, outward_right)
    )
    fourth = jnp.concatenate([left, right], axis=1)
    outward = jnp.concatenate([outward_left, outward_right], axis=1)
    mine = jnp.where(inside, third, fourth).astype(jnp.float32)
    return (mine + jnp.where(inside, second_across, outward).astype(jnp.float32)).astype(jnp.bfloat16)


def on_device(*arguments):
    if lax.axis_size("mp") == 4 and lax.axis_size("dp") == 8:
        return cube_on_device(*arguments)
    return general_on_device(*arguments)


def solution(mesh):
    placed = (
        P(("dp", "mp"), None),
        P(),
        P(None, "mp"),
        P("mp", None),
        P("dp", None, "mp"),
        P("dp", None, "mp"),
        P("dp", None),
        P("dp", None),
        P("dp"),
    )
    return jax.shard_map(
        on_device, mesh=mesh, in_specs=placed, out_specs=P(("dp", "mp"), None), check_vma=False
    )
```

```python
import functools
import math

import jax
import jax.numpy as jnp
from jax import lax
from jax.experimental import pallas as pl
from jax.experimental.pallas import tpu as pltpu
from jax.sharding import PartitionSpec as P

HD = 128
M = 64
NL = 128


def layer_norm(token_rows, norm_gain):
    values = token_rows.astype(jnp.float32)
    row_mean = jnp.mean(values, axis=-1, keepdims=True)
    centered = values - row_mean
    variance = jnp.mean(centered * centered, axis=-1, keepdims=True)
    return (centered * lax.rsqrt(variance + 1e-05) * norm_gain).astype(jnp.bfloat16)


def span_attention(queries, key_blocks, value_blocks, valid_counts, head_count):
    spans, length, local_width = queries.shape
    query_heads = queries.reshape(spans, length, head_count, HD)
    key_heads = key_blocks.reshape(spans, -1, head_count, HD)
    value_heads = value_blocks.reshape(spans, -1, head_count, HD)
    scores = jnp.einsum(
        "cmhd,ckhd->chmk", query_heads, key_heads, preferred_element_type=jnp.float32
    )
    usable = (jnp.arange(key_heads.shape[1], dtype=jnp.int32) // NL)[None, :] < valid_counts[
        :, None
    ]
    usable = usable[:, None, None, :]
    masked = jnp.where(usable, scores, -1e30)
    highest = jnp.max(masked, axis=-1, keepdims=True)
    weights = jnp.where(usable, jnp.exp(masked - highest), 0.0)
    totals = jnp.sum(weights, axis=-1) + (valid_counts == 0).astype(jnp.float32)[:, None, None]
    mixture = jnp.einsum(
        "chmk,ckhd->cmhd",
        weights.astype(jnp.bfloat16),
        value_heads,
        preferred_element_type=jnp.float32,
    )
    mixture = mixture / jnp.transpose(totals, (0, 2, 1))[..., None]
    return mixture.reshape(spans, length, local_width).astype(jnp.bfloat16)


def general_on_device(
    tokens,
    norm_gain,
    query_weight,
    output_weight,
    key_cache,
    value_cache,
    owners,
    slot_ids,
    valid_counts,
):
    dp_count = lax.axis_size("dp")
    local_width = query_weight.shape[1]
    head_count = local_width // HD
    spans = valid_counts.shape[0]
    neighbours = 2 * spans
    capacity = max(2, (neighbours + dp_count - 1) // dp_count)
    score_scale = 1.0 / math.sqrt(HD)
    normed = layer_norm(tokens, norm_gain)
    queries = (
        jnp.dot(
            lax.all_gather(normed, "mp", axis=0, tiled=True),
            query_weight,
            preferred_element_type=jnp.float32,
        )
        * score_scale
    ).astype(jnp.bfloat16)
    seq_rows = queries.shape[0]
    shifted = jnp.concatenate(
        [queries[M - 1 :], jnp.zeros((M - 1, local_width), jnp.bfloat16)], axis=0
    )
    shifted = shifted.reshape(spans, M, local_width)
    owner_list = owners.reshape(-1)
    slot_list = slot_ids.reshape(-1)
    ordinal = jnp.arange(neighbours, dtype=jnp.int32)
    earlier = (owner_list[:, None] == owner_list[None, :]) & (ordinal[None, :] < ordinal[:, None])
    position = owner_list * capacity + jnp.sum(earlier.astype(jnp.int32), axis=1)
    placed = position[None, :] == jnp.arange(dp_count * capacity, dtype=jnp.int32)[:, None]
    slot_table = jnp.sum(jnp.where(placed, slot_list[None, :], 0), axis=1).reshape(
        dp_count, capacity
    )
    incoming = lax.all_to_all(slot_table, "dp", split_axis=0, concat_axis=0, tiled=True)
    flat_slots = incoming.reshape(-1)
    sent_keys = jnp.take(key_cache, flat_slots, axis=0).reshape(dp_count, capacity, NL, local_width)
    sent_values = jnp.take(value_cache, flat_slots, axis=0).reshape(
        dp_count, capacity, NL, local_width
    )
    got_keys, got_values = (
        lax.all_to_all(sent_keys, "dp", split_axis=0, concat_axis=0, tiled=True),
        lax.all_to_all(sent_values, "dp", split_axis=0, concat_axis=0, tiled=True),
    )
    key_blocks = jnp.take(got_keys.reshape(dp_count * capacity, NL, local_width), position, axis=0)
    value_blocks = jnp.take(
        got_values.reshape(dp_count * capacity, NL, local_width), position, axis=0
    )
    key_blocks = key_blocks.reshape(spans, 2 * NL, local_width)
    value_blocks = value_blocks.reshape(spans, 2 * NL, local_width)
    attended = span_attention(shifted, key_blocks, value_blocks, valid_counts, head_count)
    flat_rows = attended.reshape(seq_rows, local_width)
    attended = jnp.concatenate(
        [jnp.zeros((M - 1, local_width), jnp.bfloat16), flat_rows[: seq_rows - M + 1]], axis=0
    )
    return lax.psum_scatter(
        jnp.dot(attended, output_weight, preferred_element_type=jnp.float32).astype(jnp.bfloat16),
        "mp",
        scatter_dimension=0,
        tiled=True,
    )


SHARD_ORDER = ((3, 2, 1, 0), (3, 2, 1, 0), (0, 1, 2, 3), (0, 1, 2, 3))
HEADS_TOGETHER = 8
SMALL = pl.CostEstimate(flops=1, bytes_accessed=1, transcendentals=0)
OUTWARD = ((1, 0), (2, 3))
INWARD = ((0, 1), (3, 2))
MIDDLE = ((1, 2), (2, 1))


def in_hbm(values):
    return pltpu.with_memory_space_constraint(values, pltpu.HBM)


def attention_kernel(step, blocks, order_ref, relative_ref, slots_ref, counts_ref, *refs):
    query_buf = refs[0]
    key_refs = refs[1:9]
    value_refs = refs[9:17]
    out_ref = refs[17]
    key_buf, value_buf, total_buf, cache_sem = refs[18:]
    shard = order_ref[step]
    rows, width = query_buf.shape
    head_count = width // HD

    def entry_of(turn):
        span = shard * blocks - 1 + turn
        index = jnp.maximum(span, 0)
        return index, jnp.where(span < 0, 0, counts_ref[index])

    def copies(turn, neighbour, slot, index):
        for kind, (source, buf) in enumerate(((key_refs, key_buf), (value_refs, value_buf))):
            yield pltpu.make_async_copy(
                source[index].at[slot],
                buf.at[turn, pl.ds(neighbour * NL, NL)],
                cache_sem.at[turn, 2 * neighbour + kind],
            )

    def fetch(turn, carry):
        entry, count = entry_of(turn)

        @pl.when(count > 0)
        def _():
            for neighbour in range(2):
                relative = relative_ref[entry * 2 + neighbour]
                slot = slots_ref[entry * 2 + neighbour]
                for index in range(8):

                    @pl.when(relative == index)
                    def _():
                        for copy in copies(turn, neighbour, slot, index):
                            copy.start()

        return carry

    lax.fori_loop(0, blocks + 1, fetch, 0)

    def attend(turn, carry):
        _, count = entry_of(turn)
        start = pl.multiple_of(turn * M, M)
        block = pl.ds(pl.multiple_of(jnp.minimum(turn, blocks - 1) * M, M), M)
        before = pl.ds(pl.multiple_of(jnp.maximum(turn - 1, 0) * M + M - 16, 16), 16)
        earlier = pl.ds(pl.multiple_of(jnp.maximum(turn - 1, 0) * M + M - 8, 8), 8)

        @pl.when(count > 0)
        def _():
            for neighbour in range(2):
                for copy in copies(turn, neighbour, 0, 0):
                    copy.wait()
            real = lax.broadcasted_iota(jnp.int32, (M, 2 * NL), 1) < count * NL
            row = lax.broadcasted_iota(jnp.int32, (16, HD), 0)
            for first_head in range(0, head_count, HEADS_TOGETHER):
                heads = [
                    pl.ds(head * HD, HD) for head in range(first_head, first_head + HEADS_TOGETHER)
                ]
                weights = []
                for columns in heads:
                    queries = query_buf[block, columns]
                    tail = jnp.where(
                        row == 15,
                        query_buf[before, columns].astype(jnp.float32),
                        queries[M - 16 :].astype(jnp.float32),
                    ).astype(jnp.bfloat16)
                    scores = lax.dot_general(
                        jnp.concatenate([queries[: M - 16], tail], axis=0),
                        key_buf[turn, :, columns],
                        (((1,), (1,)), ((), ())),
                        preferred_element_type=jnp.float32,
                    )
                    weights.append(jnp.where(real, scores, -1e30))
                weights = [jnp.exp(w - jnp.max(w, axis=-1, keepdims=True)) for w in weights]
                shares = [1.0 / jnp.sum(w, axis=-1, keepdims=True) for w in weights]
                for columns, weight, share in zip(heads, weights, shares):
                    mixture = share * jnp.dot(
                        weight.astype(jnp.bfloat16),
                        value_buf[turn, :, columns],
                        preferred_element_type=jnp.float32,
                    )
                    total_buf[pl.ds(start, M), columns] = mixture
                    total_buf[earlier, columns] = jnp.where(
                        row[8:] == 15, mixture[M - 8 :], total_buf[earlier, columns]
                    )

        @pl.when(count <= 0)
        def _():
            total_buf[pl.ds(start, M), :] = jnp.zeros((M, width), jnp.float32)
            row = lax.broadcasted_iota(jnp.int32, (8, width), 0)
            total_buf[earlier, :] = jnp.where(row == 7, 0.0, total_buf[earlier, :])

        return carry

    lax.fori_loop(0, blocks + 1, attend, 0)
    out_ref[...] = total_buf[:rows].astype(jnp.bfloat16)


def shard_attention(step, order, relative, slots, counts, queries, keys, values):
    rows, width = queries.shape
    blocks = rows // M
    anywhere = pl.BlockSpec(memory_space=pltpu.HBM)
    return pl.pallas_call(
        functools.partial(attention_kernel, step, blocks),
        out_shape=jax.ShapeDtypeStruct((rows, width), jnp.bfloat16),
        grid_spec=pltpu.PrefetchScalarGridSpec(
            num_scalar_prefetch=4,
            grid=(1,),
            in_specs=[pl.BlockSpec((rows, width), lambda i, *_: (0, 0))] + [anywhere] * 16,
            out_specs=pl.BlockSpec((rows, width), lambda i, *_: (0, 0)),
            scratch_shapes=[
                pltpu.VMEM((blocks + 1, 2 * NL, width), jnp.bfloat16),
                pltpu.VMEM((blocks + 1, 2 * NL, width), jnp.bfloat16),
                pltpu.VMEM((rows + M, width), jnp.float32),
                pltpu.SemaphoreType.DMA((blocks + 1, 4)),
            ],
        ),
        compiler_params=pltpu.CompilerParams(vmem_limit_bytes=16 << 20),
        cost_estimate=SMALL,
    )(order, relative, slots, counts, queries, *keys, *values)


def project_kernel(scale, which_ref, *refs):
    sources = refs[: len(refs) - 4]
    weight_ref, out_ref, rows_buf, sem = refs[len(refs) - 4 :]

    @pl.when(pl.program_id(0) == 0)
    def _():
        for index, source in enumerate(sources):

            @pl.when(which_ref[0] == index)
            def _():
                copy = pltpu.make_async_copy(source, rows_buf, sem)
                copy.start()
                copy.wait()

    total = jnp.dot(rows_buf[...], weight_ref[...], preferred_element_type=jnp.float32)
    out_ref[...] = (total * scale).astype(jnp.bfloat16)


def project(which, sources, weight, streamed=True):
    rows, depth = sources[0].shape
    width = weight.shape[1]
    return pl.pallas_call(
        functools.partial(project_kernel, 1.0 / math.sqrt(HD)),
        out_shape=jax.ShapeDtypeStruct((rows, width), jnp.bfloat16),
        grid_spec=pltpu.PrefetchScalarGridSpec(
            num_scalar_prefetch=1,
            grid=(width // 256,),
            in_specs=[pl.BlockSpec(memory_space=pltpu.HBM)] * len(sources)
            + [pl.BlockSpec((depth, 256), lambda i, _: (0, i))],
            out_specs=pl.BlockSpec((rows, 256), lambda i, _: (0, i)),
            scratch_shapes=[pltpu.VMEM((rows, depth), jnp.bfloat16), pltpu.SemaphoreType.DMA],
        ),
        compiler_params=pltpu.CompilerParams(vmem_limit_bytes=16 << 20),
        cost_estimate=SMALL,
    )(which.reshape(1), *sources, in_hbm(weight) if streamed else weight)


def output_kernel(core_ref, attended_ref, handed_ref, weight_ref, *refs):
    out_ref = refs[4]
    height = refs[0].shape[0]
    if weight_ref is None:
        total = attended_ref[...]
    else:
        total = jnp.dot(attended_ref[...], weight_ref[...], preferred_element_type=jnp.float32)
    for index, piece in enumerate(refs[:4]):
        from_core = core_ref[0] if index < 2 else 1 - core_ref[0]
        start = from_core * 2 * height + index % 2 * height
        heads = handed_ref[:, pl.ds(pl.multiple_of(start, height), height)]
        total += jnp.dot(heads, piece[...], preferred_element_type=jnp.float32)
    out_ref[...] = total.astype(jnp.bfloat16)


def output_rest_kernel(core_ref, part_ref, handed_ref, *refs):
    output_kernel(core_ref, part_ref, handed_ref, None, *refs)


def output_plus_kernel(attended_ref, weight_ref, plus_ref, out_ref):
    total = jnp.dot(attended_ref[...], weight_ref[...], preferred_element_type=jnp.float32)
    out_ref[...] = (total + plus_ref[...].astype(jnp.float32)).astype(jnp.bfloat16)


def output_only_kernel(attended_ref, weight_ref, out_ref):
    out_ref[...] = jnp.dot(attended_ref[...], weight_ref[...], preferred_element_type=jnp.float32)


def fixed_block(rows, depth):
    return pl.BlockSpec((rows, depth), lambda i, *_: (0, 0))


def column_block(height, start):
    return pl.BlockSpec((height, 512), lambda i, *_: (0, start + i))


def output_call(kernel, prefetched, in_specs, rows, count, kind, *operands):
    return pl.pallas_call(
        kernel,
        out_shape=jax.ShapeDtypeStruct((rows, count * 512), kind),
        grid_spec=pltpu.PrefetchScalarGridSpec(
            num_scalar_prefetch=prefetched,
            grid=(count,),
            in_specs=in_specs,
            out_specs=column_block(rows, 0),
        ),
        compiler_params=pltpu.CompilerParams(vmem_limit_bytes=16 << 20),
        cost_estimate=SMALL,
    )(*operands)


def output_part(core, attended, handed, weight, inner, first, count):
    rows, depth = handed.shape
    inner = [in_hbm(piece) for piece in inner]
    pieces = [column_block(piece.shape[0], first) for piece in inner]
    return output_call(
        output_kernel,
        1,
        [fixed_block(rows, depth), fixed_block(rows, depth), column_block(depth, first)] + pieces,
        rows,
        count,
        jnp.bfloat16,
        core.reshape(1),
        attended,
        handed,
        in_hbm(weight),
        *inner,
    )


def output_rest(core, part, handed, inner, first, count):
    rows, depth = handed.shape
    inner = [in_hbm(piece) for piece in inner]
    pieces = [column_block(piece.shape[0], first) for piece in inner]
    return output_call(
        output_rest_kernel,
        1,
        [column_block(rows, 0), fixed_block(rows, depth)] + pieces,
        rows,
        count,
        jnp.bfloat16,
        core.reshape(1),
        part,
        handed,
        *inner,
    )


def output_only(attended, weight, first, count):
    rows, depth = attended.shape
    return output_call(
        output_only_kernel,
        0,
        [fixed_block(rows, depth), column_block(depth, first)],
        rows,
        count,
        jnp.float32,
        attended,
        in_hbm(weight),
    )


def output_plus(attended, weight, plus, first, count):
    rows, depth = attended.shape
    return output_call(
        output_plus_kernel,
        0,
        [fixed_block(rows, depth), column_block(depth, first), column_block(rows, 0)],
        rows,
        count,
        jnp.bfloat16,
        attended,
        in_hbm(weight),
        plus,
    )


def swap(values, bits):
    return lax.ppermute(values, "dp", [(i, i ^ bits) for i in range(8)])


def along(values, pairs):
    return lax.ppermute(values, "mp", list(pairs))


def cube_on_device(
    tokens,
    norm_gain,
    query_weight,
    output_weight,
    key_cache,
    value_cache,
    owners,
    slot_ids,
    valid_counts,
):
    place = lax.axis_index("mp")

    together = lax.optimization_barrier
    core = lax.axis_index("dp") % 2
    half = output_weight.shape[0] // 2
    inside = (place == 1) | (place == 2)
    keys, values = [key_cache] + [None] * 7, [value_cache] + [None] * 7
    normed = layer_norm(tokens, norm_gain)
    beside = along(normed, INWARD + OUTWARD)
    middle = along(normed, MIDDLE)
    keys_x, values_y = swap(key_cache, 2), swap(value_cache, 4)
    keys[1] = swap(key_cache, 1)
    keys[1], value_source = together((keys[1], value_cache))
    values[1] = swap(value_source, 1)
    handed = [
        lax.dynamic_slice_in_dim(output_weight, core * half + start, half // 2, 0) for start in (0, half // 2)
    ]
    order, third_from, fourth_from, second_from, first_from = (
        lax.dynamic_index_in_dim(jnp.array(table, jnp.int32), place, 0, keepdims=False)
        for table in (SHARD_ORDER, (1, 0, 0, 1), (0, 1, 1, 0), (0, 1, 1, 0), (1, 0, 0, 1))
    )
    relative = owners.reshape(-1) ^ lax.axis_index("dp")
    slots = slot_ids.reshape(-1)
    beside, middle, handed, keys[1], values[1], order, relative, slots, keys_x, values_y, keys_far, values_far = (
        together(
            (
                beside,
                middle,
                handed,
                keys[1],
                values[1],
                order,
                relative,
                slots,
                keys_x,
                values_y,
                key_cache,
                value_cache,
            )
        )
    )
    beside_two = along(beside, MIDDLE)
    middle_two = along(middle, OUTWARD)
    keys_y, values_x = swap(keys_far, 4), swap(values_far, 2)
    inner = [along(handed[0], INWARD)]
    third_queries = project(third_from, (normed, beside), query_weight)
    fourth_queries = project(fourth_from, (normed, beside), query_weight)
    beside_two, middle_two, keys_y, values_x, keys_x, values_y, third_queries, fourth_queries, handed, inner = (
        together(
            (
                beside_two,
                middle_two,
                keys_y,
                values_x,
                keys_x,
                values_y,
                third_queries,
                fourth_queries,
                handed,
                inner,
            )
        )
    )
    keys[2], values[4], keys[4], values[2] = keys_x, values_y, keys_y, values_x
    three = along(beside_two, OUTWARD)
    keys[6], values[6] = swap(keys_x, 4), swap(values_y, 2)
    inner += [along(handed[1], INWARD)]
    second_queries = project(second_from, (middle_two, middle), query_weight)
    keys[3], values[5] = swap(keys_x, 1), swap(values_y, 1)
    keys[3], keys_y, values_x, second_queries = together((keys[3], keys_y, values_x, second_queries))
    keys[5], values[3] = swap(keys_y, 1), swap(values_x, 1)
    three, keys[6], values[6], inner = together((three, keys[6], values[6], inner))
    keys[7], values[7] = swap(keys[6], 1), swap(values[6], 1)
    first_queries = project(first_from, (beside_two, three), query_weight, streamed=False)

    def attend(step, queries):
        return shard_attention(step, order, relative, slots, valid_counts, queries, keys, values)

    def output(attended, handed, first, count):
        return output_part(core, attended, handed, output_weight, inner, first, count)

    tiles = output_weight.shape[1] // 512
    first = attend(0, first_queries)
    first_in = along(first, INWARD)
    first, second_queries, inner = together((first, second_queries, inner))
    inner += [swap(piece, 1) for piece in inner]
    left = output_only(first, output_weight, 0, tiles // 2)
    left, second_queries = together((left, second_queries))
    second = attend(1, second_queries)
    second_in = along(second, INWARD)
    first_in, second = together((first_in, second))
    left = output_rest(core, left, first_in, inner, 0, tiles // 2)
    across_left = along(left, MIDDLE)
    _, first, first_in = together((left, first, first_in))
    right = output(first, first_in, tiles // 2, tiles // 2)
    across_right = along(right, MIDDLE)
    _, fourth_queries = together((right, fourth_queries))
    fourth = attend(3, fourth_queries)
    fourth, third_queries = together((fourth, third_queries))
    third = attend(2, third_queries)
    third_in = along(third, INWARD)
    _, fourth, across_left = together((third, fourth, across_left))
    left = output_plus(fourth, output_weight, across_left, 0, tiles // 2)
    outward_left = along(left, OUTWARD)
    _, second, second_in = together((left, second, second_in))
    second = output(second, second_in, 0, tiles)
    second_across = along(second, MIDDLE)
    _, fourth, across_right, outward_left, third_in = together(
        (second, fourth, across_right, outward_left, third_in)
    )
    right = output_plus(fourth, output_weight, across_right, tiles // 2, tiles // 2)
    outward_right = along(right, OUTWARD)
    _, third, third_in = together((right, third, third_in))
    third = output(third, third_in, 0, tiles)
    third, second_across, outward_left, outward_right = together(
        (third, second_across, outward_left, outward_right)
    )
    fourth = jnp.concatenate([left, right], axis=1)
    outward = jnp.concatenate([outward_left, outward_right], axis=1)
    mine = jnp.where(inside, third, fourth).astype(jnp.float32)
    return (mine + jnp.where(inside, second_across, outward).astype(jnp.float32)).astype(jnp.bfloat16)


def on_device(*arguments):
    if lax.axis_size("mp") == 4 and lax.axis_size("dp") == 8:
        return cube_on_device(*arguments)
    return general_on_device(*arguments)


def solution(mesh):
    placed = (
        P(("dp", "mp"), None),
        P(),
        P(None, "mp"),
        P("mp", None),
        P("dp", None, "mp"),
        P("dp", None, "mp"),
        P("dp", None),
        P("dp", None),
        P("dp"),
    )
    return jax.shard_map(
        on_device, mesh=mesh, in_specs=placed, out_specs=P(("dp", "mp"), None), check_vma=False
    )
```

```python
import functools
import math

import jax
import jax.numpy as jnp
from jax import lax
from jax.experimental import pallas as pl
from jax.experimental.pallas import tpu as pltpu
from jax.sharding import PartitionSpec as P

HD = 128
M = 64
NL = 128


def layer_norm(token_rows, norm_gain):
    values = token_rows.astype(jnp.float32)
    row_mean = jnp.mean(values, axis=-1, keepdims=True)
    centered = values - row_mean
    variance = jnp.mean(centered * centered, axis=-1, keepdims=True)
    return (centered * lax.rsqrt(variance + 1e-05) * norm_gain).astype(jnp.bfloat16)


def span_attention(queries, key_blocks, value_blocks, valid_counts, head_count):
    spans, length, local_width = queries.shape
    query_heads = queries.reshape(spans, length, head_count, HD)
    key_heads = key_blocks.reshape(spans, -1, head_count, HD)
    value_heads = value_blocks.reshape(spans, -1, head_count, HD)
    scores = jnp.einsum(
        "cmhd,ckhd->chmk", query_heads, key_heads, preferred_element_type=jnp.float32
    )
    usable = (jnp.arange(key_heads.shape[1], dtype=jnp.int32) // NL)[None, :] < valid_counts[
        :, None
    ]
    usable = usable[:, None, None, :]
    masked = jnp.where(usable, scores, -1e30)
    highest = jnp.max(masked, axis=-1, keepdims=True)
    weights = jnp.where(usable, jnp.exp(masked - highest), 0.0)
    totals = jnp.sum(weights, axis=-1) + (valid_counts == 0).astype(jnp.float32)[:, None, None]
    mixture = jnp.einsum(
        "chmk,ckhd->cmhd",
        weights.astype(jnp.bfloat16),
        value_heads,
        preferred_element_type=jnp.float32,
    )
    mixture = mixture / jnp.transpose(totals, (0, 2, 1))[..., None]
    return mixture.reshape(spans, length, local_width).astype(jnp.bfloat16)


def general_on_device(
    tokens,
    norm_gain,
    query_weight,
    output_weight,
    key_cache,
    value_cache,
    owners,
    slot_ids,
    valid_counts,
):
    dp_count = lax.axis_size("dp")
    local_width = query_weight.shape[1]
    head_count = local_width // HD
    spans = valid_counts.shape[0]
    neighbours = 2 * spans
    capacity = max(2, (neighbours + dp_count - 1) // dp_count)
    score_scale = 1.0 / math.sqrt(HD)
    normed = layer_norm(tokens, norm_gain)
    queries = (
        jnp.dot(
            lax.all_gather(normed, "mp", axis=0, tiled=True),
            query_weight,
            preferred_element_type=jnp.float32,
        )
        * score_scale
    ).astype(jnp.bfloat16)
    seq_rows = queries.shape[0]
    shifted = jnp.concatenate(
        [queries[M - 1 :], jnp.zeros((M - 1, local_width), jnp.bfloat16)], axis=0
    )
    shifted = shifted.reshape(spans, M, local_width)
    owner_list = owners.reshape(-1)
    slot_list = slot_ids.reshape(-1)
    ordinal = jnp.arange(neighbours, dtype=jnp.int32)
    earlier = (owner_list[:, None] == owner_list[None, :]) & (ordinal[None, :] < ordinal[:, None])
    position = owner_list * capacity + jnp.sum(earlier.astype(jnp.int32), axis=1)
    placed = position[None, :] == jnp.arange(dp_count * capacity, dtype=jnp.int32)[:, None]
    slot_table = jnp.sum(jnp.where(placed, slot_list[None, :], 0), axis=1).reshape(
        dp_count, capacity
    )
    incoming = lax.all_to_all(slot_table, "dp", split_axis=0, concat_axis=0, tiled=True)
    flat_slots = incoming.reshape(-1)
    sent_keys = jnp.take(key_cache, flat_slots, axis=0).reshape(dp_count, capacity, NL, local_width)
    sent_values = jnp.take(value_cache, flat_slots, axis=0).reshape(
        dp_count, capacity, NL, local_width
    )
    got_keys, got_values = (
        lax.all_to_all(sent_keys, "dp", split_axis=0, concat_axis=0, tiled=True),
        lax.all_to_all(sent_values, "dp", split_axis=0, concat_axis=0, tiled=True),
    )
    key_blocks = jnp.take(got_keys.reshape(dp_count * capacity, NL, local_width), position, axis=0)
    value_blocks = jnp.take(
        got_values.reshape(dp_count * capacity, NL, local_width), position, axis=0
    )
    key_blocks = key_blocks.reshape(spans, 2 * NL, local_width)
    value_blocks = value_blocks.reshape(spans, 2 * NL, local_width)
    attended = span_attention(shifted, key_blocks, value_blocks, valid_counts, head_count)
    flat_rows = attended.reshape(seq_rows, local_width)
    attended = jnp.concatenate(
        [jnp.zeros((M - 1, local_width), jnp.bfloat16), flat_rows[: seq_rows - M + 1]], axis=0
    )
    return lax.psum_scatter(
        jnp.dot(attended, output_weight, preferred_element_type=jnp.float32).astype(jnp.bfloat16),
        "mp",
        scatter_dimension=0,
        tiled=True,
    )


SHARD_ORDER = ((3, 2, 1, 0), (3, 2, 1, 0), (0, 1, 2, 3), (0, 1, 2, 3))
HEADS_TOGETHER = 8
SMALL = pl.CostEstimate(flops=1, bytes_accessed=1, transcendentals=0)
OUTWARD = ((1, 0), (2, 3))
INWARD = ((0, 1), (3, 2))
MIDDLE = ((1, 2), (2, 1))


def in_hbm(values):
    return pltpu.with_memory_space_constraint(values, pltpu.HBM)


def attention_kernel(step, blocks, order_ref, relative_ref, slots_ref, counts_ref, *refs):
    query_buf = refs[0]
    key_refs = refs[1:9]
    value_refs = refs[9:17]
    out_ref = refs[17]
    key_buf, value_buf, total_buf, cache_sem = refs[18:]
    shard = order_ref[step]
    rows, width = query_buf.shape
    head_count = width // HD

    def entry_of(turn):
        span = shard * blocks - 1 + turn
        index = jnp.maximum(span, 0)
        return index, jnp.where(span < 0, 0, counts_ref[index])

    def copies(turn, neighbour, slot, index):
        for kind, (source, buf) in enumerate(((key_refs, key_buf), (value_refs, value_buf))):
            yield pltpu.make_async_copy(
                source[index].at[slot],
                buf.at[turn, pl.ds(neighbour * NL, NL)],
                cache_sem.at[turn, 2 * neighbour + kind],
            )

    def fetch(turn, carry):
        entry, count = entry_of(turn)

        @pl.when(count > 0)
        def _():
            for neighbour in range(2):
                relative = relative_ref[entry * 2 + neighbour]
                slot = slots_ref[entry * 2 + neighbour]
                for index in range(8):

                    @pl.when(relative == index)
                    def _():
                        for copy in copies(turn, neighbour, slot, index):
                            copy.start()

        return carry

    lax.fori_loop(0, blocks + 1, fetch, 0)

    def attend(turn, carry):
        _, count = entry_of(turn)
        start = pl.multiple_of(turn * M, M)
        block = pl.ds(pl.multiple_of(jnp.minimum(turn, blocks - 1) * M, M), M)
        before = pl.ds(pl.multiple_of(jnp.maximum(turn - 1, 0) * M + M - 16, 16), 16)
        earlier = pl.ds(pl.multiple_of(jnp.maximum(turn - 1, 0) * M + M - 8, 8), 8)

        @pl.when(count > 0)
        def _():
            for neighbour in range(2):
                for copy in copies(turn, neighbour, 0, 0):
                    copy.wait()
            real = lax.broadcasted_iota(jnp.int32, (M, 2 * NL), 1) < count * NL
            row = lax.broadcasted_iota(jnp.int32, (16, HD), 0)
            for first_head in range(0, head_count, HEADS_TOGETHER):
                heads = [
                    pl.ds(head * HD, HD) for head in range(first_head, first_head + HEADS_TOGETHER)
                ]
                weights = []
                for columns in heads:
                    queries = query_buf[block, columns]
                    tail = jnp.where(
                        row == 15,
                        query_buf[before, columns].astype(jnp.float32),
                        queries[M - 16 :].astype(jnp.float32),
                    ).astype(jnp.bfloat16)
                    scores = lax.dot_general(
                        jnp.concatenate([queries[: M - 16], tail], axis=0),
                        key_buf[turn, :, columns],
                        (((1,), (1,)), ((), ())),
                        preferred_element_type=jnp.float32,
                    )
                    weights.append(jnp.where(real, scores, -1e30))
                weights = [jnp.exp(w - jnp.max(w, axis=-1, keepdims=True)) for w in weights]
                shares = [1.0 / jnp.sum(w, axis=-1, keepdims=True) for w in weights]
                for columns, weight, share in zip(heads, weights, shares):
                    mixture = share * jnp.dot(
                        weight.astype(jnp.bfloat16),
                        value_buf[turn, :, columns],
                        preferred_element_type=jnp.float32,
                    )
                    total_buf[pl.ds(start, M), columns] = mixture
                    total_buf[earlier, columns] = jnp.where(
                        row[8:] == 15, mixture[M - 8 :], total_buf[earlier, columns]
                    )

        @pl.when(count <= 0)
        def _():
            total_buf[pl.ds(start, M), :] = jnp.zeros((M, width), jnp.float32)
            row = lax.broadcasted_iota(jnp.int32, (8, width), 0)
            total_buf[earlier, :] = jnp.where(row == 7, 0.0, total_buf[earlier, :])

        return carry

    lax.fori_loop(0, blocks + 1, attend, 0)
    out_ref[...] = total_buf[:rows].astype(jnp.bfloat16)


def shard_attention(step, order, relative, slots, counts, queries, keys, values):
    rows, width = queries.shape
    blocks = rows // M
    anywhere = pl.BlockSpec(memory_space=pltpu.HBM)
    return pl.pallas_call(
        functools.partial(attention_kernel, step, blocks),
        out_shape=jax.ShapeDtypeStruct((rows, width), jnp.bfloat16),
        grid_spec=pltpu.PrefetchScalarGridSpec(
            num_scalar_prefetch=4,
            grid=(1,),
            in_specs=[pl.BlockSpec((rows, width), lambda i, *_: (0, 0))] + [anywhere] * 16,
            out_specs=pl.BlockSpec((rows, width), lambda i, *_: (0, 0)),
            scratch_shapes=[
                pltpu.VMEM((blocks + 1, 2 * NL, width), jnp.bfloat16),
                pltpu.VMEM((blocks + 1, 2 * NL, width), jnp.bfloat16),
                pltpu.VMEM((rows + M, width), jnp.float32),
                pltpu.SemaphoreType.DMA((blocks + 1, 4)),
            ],
        ),
        compiler_params=pltpu.CompilerParams(vmem_limit_bytes=13 << 20),
        cost_estimate=SMALL,
    )(order, relative, slots, counts, queries, *keys, *values)


def project_kernel(scale, which_ref, *refs):
    sources = refs[: len(refs) - 4]
    weight_ref, out_ref, rows_buf, sem = refs[len(refs) - 4 :]

    @pl.when(pl.program_id(0) == 0)
    def _():
        for index, source in enumerate(sources):

            @pl.when(which_ref[0] == index)
            def _():
                copy = pltpu.make_async_copy(source, rows_buf, sem)
                copy.start()
                copy.wait()

    total = jnp.dot(rows_buf[...], weight_ref[...], preferred_element_type=jnp.float32)
    out_ref[...] = (total * scale).astype(jnp.bfloat16)


def project(which, sources, weight, streamed=True):
    rows, depth = sources[0].shape
    width = weight.shape[1]
    return pl.pallas_call(
        functools.partial(project_kernel, 1.0 / math.sqrt(HD)),
        out_shape=jax.ShapeDtypeStruct((rows, width), jnp.bfloat16),
        grid_spec=pltpu.PrefetchScalarGridSpec(
            num_scalar_prefetch=1,
            grid=(width // 256,),
            in_specs=[pl.BlockSpec(memory_space=pltpu.HBM)] * len(sources)
            + [pl.BlockSpec((depth, 256), lambda i, _: (0, i))],
            out_specs=pl.BlockSpec((rows, 256), lambda i, _: (0, i)),
            scratch_shapes=[pltpu.VMEM((rows, depth), jnp.bfloat16), pltpu.SemaphoreType.DMA],
        ),
        compiler_params=pltpu.CompilerParams(vmem_limit_bytes=13 << 20),
        cost_estimate=SMALL,
    )(which.reshape(1), *sources, in_hbm(weight) if streamed else weight)


def output_kernel(core_ref, attended_ref, handed_ref, weight_ref, *refs):
    out_ref = refs[4]
    height = refs[0].shape[0]
    if weight_ref is None:
        total = attended_ref[...]
    else:
        total = jnp.dot(attended_ref[...], weight_ref[...], preferred_element_type=jnp.float32)
    for index, piece in enumerate(refs[:4]):
        from_core = core_ref[0] if index < 2 else 1 - core_ref[0]
        start = from_core * 2 * height + index % 2 * height
        heads = handed_ref[:, pl.ds(pl.multiple_of(start, height), height)]
        total += jnp.dot(heads, piece[...], preferred_element_type=jnp.float32)
    out_ref[...] = total.astype(jnp.bfloat16)


def output_rest_kernel(core_ref, part_ref, handed_ref, *refs):
    output_kernel(core_ref, part_ref, handed_ref, None, *refs)


def output_plus_kernel(attended_ref, weight_ref, plus_ref, out_ref):
    total = jnp.dot(attended_ref[...], weight_ref[...], preferred_element_type=jnp.float32)
    out_ref[...] = (total + plus_ref[...].astype(jnp.float32)).astype(jnp.bfloat16)


def output_only_kernel(attended_ref, weight_ref, out_ref):
    out_ref[...] = jnp.dot(attended_ref[...], weight_ref[...], preferred_element_type=jnp.float32)


def fixed_block(rows, depth):
    return pl.BlockSpec((rows, depth), lambda i, *_: (0, 0))


def column_block(height, start):
    return pl.BlockSpec((height, 512), lambda i, *_: (0, start + i))


def output_call(kernel, prefetched, in_specs, rows, count, kind, *operands):
    return pl.pallas_call(
        kernel,
        out_shape=jax.ShapeDtypeStruct((rows, count * 512), kind),
        grid_spec=pltpu.PrefetchScalarGridSpec(
            num_scalar_prefetch=prefetched,
            grid=(count,),
            in_specs=in_specs,
            out_specs=column_block(rows, 0),
        ),
        compiler_params=pltpu.CompilerParams(vmem_limit_bytes=13 << 20),
        cost_estimate=SMALL,
    )(*operands)


def output_part(core, attended, handed, weight, inner, first, count):
    rows, depth = handed.shape
    inner = [in_hbm(piece) for piece in inner]
    pieces = [column_block(piece.shape[0], first) for piece in inner]
    return output_call(
        output_kernel,
        1,
        [fixed_block(rows, depth), fixed_block(rows, depth), column_block(depth, first)] + pieces,
        rows,
        count,
        jnp.bfloat16,
        core.reshape(1),
        attended,
        handed,
        in_hbm(weight),
        *inner,
    )


def output_rest(core, part, handed, inner, first, count):
    rows, depth = handed.shape
    inner = [in_hbm(piece) for piece in inner]
    pieces = [column_block(piece.shape[0], first) for piece in inner]
    return output_call(
        output_rest_kernel,
        1,
        [column_block(rows, 0), fixed_block(rows, depth)] + pieces,
        rows,
        count,
        jnp.bfloat16,
        core.reshape(1),
        part,
        handed,
        *inner,
    )


def output_only(attended, weight, first, count):
    rows, depth = attended.shape
    return output_call(
        output_only_kernel,
        0,
        [fixed_block(rows, depth), column_block(depth, first)],
        rows,
        count,
        jnp.float32,
        attended,
        in_hbm(weight),
    )


def output_plus(attended, weight, plus, first, count):
    rows, depth = attended.shape
    return output_call(
        output_plus_kernel,
        0,
        [fixed_block(rows, depth), column_block(depth, first), column_block(rows, 0)],
        rows,
        count,
        jnp.bfloat16,
        attended,
        in_hbm(weight),
        plus,
    )


def swap(values, bits):
    return lax.ppermute(values, "dp", [(i, i ^ bits) for i in range(8)])


def along(values, pairs):
    return lax.ppermute(values, "mp", list(pairs))


def cube_on_device(
    tokens,
    norm_gain,
    query_weight,
    output_weight,
    key_cache,
    value_cache,
    owners,
    slot_ids,
    valid_counts,
):
    place = lax.axis_index("mp")

    together = lax.optimization_barrier
    core = lax.axis_index("dp") % 2
    half = output_weight.shape[0] // 2
    inside = (place == 1) | (place == 2)
    keys, values = [key_cache] + [None] * 7, [value_cache] + [None] * 7
    normed = layer_norm(tokens, norm_gain)
    beside = along(normed, INWARD + OUTWARD)
    middle = along(normed, MIDDLE)
    keys_x, values_y = swap(key_cache, 2), swap(value_cache, 4)
    keys[1] = swap(key_cache, 1)
    keys[1], value_source = together((keys[1], value_cache))
    values[1] = swap(value_source, 1)
    handed = [
        lax.dynamic_slice_in_dim(output_weight, core * half + start, half // 2, 0) for start in (0, half // 2)
    ]
    order, third_from, fourth_from, second_from, first_from = (
        lax.dynamic_index_in_dim(jnp.array(table, jnp.int32), place, 0, keepdims=False)
        for table in (SHARD_ORDER, (1, 0, 0, 1), (0, 1, 1, 0), (0, 1, 1, 0), (1, 0, 0, 1))
    )
    relative = owners.reshape(-1) ^ lax.axis_index("dp")
    slots = slot_ids.reshape(-1)
    beside, middle, handed, keys[1], values[1], order, relative, slots, keys_x, values_y, keys_far, values_far = (
        together(
            (
                beside,
                middle,
                handed,
                keys[1],
                values[1],
                order,
                relative,
                slots,
                keys_x,
                values_y,
                key_cache,
                value_cache,
            )
        )
    )
    beside_two = along(beside, MIDDLE)
    middle_two = along(middle, OUTWARD)
    keys_y, values_x = swap(keys_far, 4), swap(values_far, 2)
    inner = [along(handed[0], INWARD)]
    third_queries = project(third_from, (normed, beside), query_weight)
    fourth_queries = project(fourth_from, (normed, beside), query_weight)
    beside_two, middle_two, keys_y, values_x, keys_x, values_y, third_queries, fourth_queries, handed, inner = (
        together(
            (
                beside_two,
                middle_two,
                keys_y,
                values_x,
                keys_x,
                values_y,
                third_queries,
                fourth_queries,
                handed,
                inner,
            )
        )
    )
    keys[2], values[4], keys[4], values[2] = keys_x, values_y, keys_y, values_x
    three = along(beside_two, OUTWARD)
    keys[6], values[6] = swap(keys_x, 4), swap(values_y, 2)
    inner += [along(handed[1], INWARD)]
    second_queries = project(second_from, (middle_two, middle), query_weight)
    keys[3], values[5] = swap(keys_x, 1), swap(values_y, 1)
    keys[3], keys_y, values_x, second_queries = together((keys[3], keys_y, values_x, second_queries))
    keys[5], values[3] = swap(keys_y, 1), swap(values_x, 1)
    three, keys[6], values[6], inner = together((three, keys[6], values[6], inner))
    keys[7], values[7] = swap(keys[6], 1), swap(values[6], 1)
    first_queries = project(first_from, (beside_two, three), query_weight, streamed=False)

    def attend(step, queries):
        return shard_attention(step, order, relative, slots, valid_counts, queries, keys, values)

    def output(attended, handed, first, count):
        return output_part(core, attended, handed, output_weight, inner, first, count)

    tiles = output_weight.shape[1] // 512
    first = attend(0, first_queries)
    first_in = along(first, INWARD)
    first, second_queries, inner = together((first, second_queries, inner))
    inner += [swap(piece, 1) for piece in inner]
    left = output_only(first, output_weight, 0, tiles // 2)
    left, second_queries = together((left, second_queries))
    second = attend(1, second_queries)
    second_in = along(second, INWARD)
    first_in, second = together((first_in, second))
    left = output_rest(core, left, first_in, inner, 0, tiles // 2)
    across_left = along(left, MIDDLE)
    _, first, first_in = together((left, first, first_in))
    right = output(first, first_in, tiles // 2, tiles // 2)
    across_right = along(right, MIDDLE)
    _, fourth_queries = together((right, fourth_queries))
    fourth = attend(3, fourth_queries)
    fourth, third_queries = together((fourth, third_queries))
    third = attend(2, third_queries)
    third_in = along(third, INWARD)
    _, second, second_in = together((third, second, second_in))
    second = output(second, second_in, 0, tiles)
    second_across = along(second, MIDDLE)
    _, fourth, across_left = together((second, fourth, across_left))
    left = output_plus(fourth, output_weight, across_left, 0, tiles // 2)
    outward_left = along(left, OUTWARD)
    fourth, across_right, outward_left, third_in = together((fourth, across_right, outward_left, third_in))
    right = output_plus(fourth, output_weight, across_right, tiles // 2, tiles // 2)
    outward_right = along(right, OUTWARD)
    _, third, third_in = together((right, third, third_in))
    third = output(third, third_in, 0, tiles)
    third, second_across, outward_left, outward_right = together(
        (third, second_across, outward_left, outward_right)
    )
    fourth = jnp.concatenate([left, right], axis=1)
    outward = jnp.concatenate([outward_left, outward_right], axis=1)
    mine = jnp.where(inside, third, fourth).astype(jnp.float32)
    return (mine + jnp.where(inside, second_across, outward).astype(jnp.float32)).astype(jnp.bfloat16)


def on_device(*arguments):
    if lax.axis_size("mp") == 4 and lax.axis_size("dp") == 8:
        return cube_on_device(*arguments)
    return general_on_device(*arguments)


def solution(mesh):
    placed = (
        P(("dp", "mp"), None),
        P(),
        P(None, "mp"),
        P("mp", None),
        P("dp", None, "mp"),
        P("dp", None, "mp"),
        P("dp", None),
        P("dp", None),
        P("dp"),
    )
    return jax.shard_map(
        on_device, mesh=mesh, in_specs=placed, out_specs=P(("dp", "mp"), None), check_vma=False
    )
```
